512 devices in a mesh: seq: 32 (over z, y_hi), chan: 8 (over x, y_lo), dp: 2 (over core).
Axes of the slice: x: 4, y: 8 (y_hi: 4, y_lo: 2; y = y_hi * 2 + y_lo), z: 8, core: 2. Of those that a mesh axis runs over, the one named last changes fastest.
Arguments:
- hidden: bfloat16 [8192, 2048], P(('dp', 'seq')), parts along dimension 0, may hold values from -6 to 6
- complement: bfloat16 [8192, 2048], P(('dp', 'seq')), parts along dimension 0, may hold values from -6 to 6
- inner_weight: bfloat16 [2048, 4096], P(None, 'chan'), may hold values from -0.125 to 0.125
- select_weight: bfloat16 [2048, 256], replicated, may hold values from -0.015625 to 0.015625
- step_weight: bfloat16 [2048, 64], P(None, 'chan'), may hold values from -0.125 to 0.125
- step_bias: float32 [64], P('chan'), may hold values from -4 to -2
- decay_rate: float32 [64], P('chan'), as said below
- skip_gain: float32 [64], P('chan'), may hold values from 0.5 to 2
- cotangent: bfloat16 [8192, 4096], P(('dp', 'seq'), 'chan'), parts along dimension 0, may hold values from -6 to 6
- complement_cotangent: bfloat16 [8192, 4096], P(('dp', 'seq'), 'chan'), parts along dimension 0, may hold values from -6 to 6
Outputs:
- mixed: bfloat16 [8192, 4096], P(('dp', 'seq'), 'chan'), parts along dimension 0
- mixed_complement: bfloat16 [8192, 4096], P(('dp', 'seq'), 'chan'), parts along dimension 0
- grad_hidden: bfloat16 [8192, 2048], P(('dp', 'seq'), 'chan'), parts along dimension 0
- grad_complement: bfloat16 [8192, 2048], P(('dp', 'seq'), 'chan'), parts along dimension 0
The draws below stay inside these ranges and needn't reach their ends.
There are 2 independent parts, one for each index of `dp`. The reference program is written for one: setup_inputs(seed, part) draws one part's arguments, and reference() takes and returns one part's arrays. A program takes and returns all parts, laid end to end along the dimension named above; an argument that names none is the same for every part. Nothing has to cross between parts.
Inputs may be any that keep to these rules, and one draw needn't show every extreme that they name: `decay_rate`: each head's decay rate lies between 7 / 4096 and 0.5.
All inputs are finite; a program needn't handle non-finite values.
Results may differ from the reference program's by a relative error of at most 0.006.
Values sent between devices are 32-bit elements; how exact they have to be, the bound alone decides.
A program may use at most 192 MiB of HBM per device.

```python
import math
import jax
import jax.numpy as jnp
from jax import lax

D = 2048
HEAD_DIM = 64
STATE = 128
RD = 128
INNER = 4096
HEADS = 64
SEQ_LEN = 4096


def draw_decay_rate(key, part):
    pick_key, fast_key, slow_key = jax.random.split(key, 3)
    fast_share = 0.5
    chosen = jax.random.uniform(pick_key, (HEADS,)) < fast_share
    fast_rate = jnp.exp(jax.random.uniform(fast_key, (HEADS,), minval=math.log(0.3), maxval=math.log(0.5)))
    slow_rate = jnp.exp(jax.random.uniform(slow_key, (HEADS,), minval=math.log(7.0), maxval=math.log(28.0))) / SEQ_LEN
    return jnp.where(chosen, fast_rate, slow_rate).astype(jnp.float32)


def shard_levels(rng, dims, shards, low, largest):
    factor_of = 1.0
    for axis_at, parts in shards:
        heights = jax.random.uniform(jax.random.fold_in(jax.random.fold_in(rng, 6), axis_at), (parts,), jnp.float32, low / len(shards), largest / len(shards))
        factor_of = factor_of * jnp.repeat(jnp.exp(heights), dims[axis_at] // parts).reshape((-1,) + (1,) * (len(dims) - 1 - axis_at))
    return factor_of


def gaussian(stream_key, dims, deviation, most, pieces=(), held_as=jnp.bfloat16):
    level = shard_levels(stream_key, dims, pieces, -0.22, 0.18) if pieces else 1.0
    drawn = jax.random.normal(stream_key, dims, jnp.float32) * deviation * level
    return jnp.minimum(jnp.maximum(drawn, -most), most).astype(held_as)


def setup_inputs(seed: int = 0, part: int = 0) -> dict:
    arg_keys = jax.random.split(jax.random.key(seed), 11)
    part_splits = jax.random.split(jax.random.fold_in(arg_keys[10], part), 11)
    hidden = gaussian(part_splits[0], (SEQ_LEN, D), 1.0, 6.0, ((0, 32),))
    complement = gaussian(part_splits[1], (SEQ_LEN, D), 1.0, 6.0, ((0, 32),))
    inner_weight = gaussian(arg_keys[2], (D, INNER), D ** -0.5, 0.125, ((1, 8),))
    select_weight = gaussian(arg_keys[3], (D, 2 * STATE), (64 * D) ** -0.5, 0.015625)
    step_weight = gaussian(arg_keys[4], (D, HEADS), D ** -0.5, 0.125, ((1, 8),))
    step_bias = jnp.clip(-4.0 + 2.0 * jax.random.uniform(arg_keys[5], (HEADS,), jnp.float32) ** shard_levels(arg_keys[5], (HEADS,), ((0, 8),), -0.2, 0.2), -4.0, -2.0)
    decay_rate = draw_decay_rate(jax.random.fold_in(arg_keys[10], 71), part)
    skip_gain = jnp.clip(jnp.exp(math.log(2.0) - 1.3862944 * jax.random.uniform(arg_keys[7], (HEADS,), jnp.float32) ** shard_levels(arg_keys[7], (HEADS,), ((0, 8),), -0.2, 0.2)), 0.5, 2.0)
    cotangent = gaussian(part_splits[8], (SEQ_LEN, INNER), 1.0, 6.0, ((0, 32), (1, 8)))
    complement_cotangent = gaussian(part_splits[9], (SEQ_LEN, INNER), 1.0, 6.0, ((0, 32), (1, 8)))
    return {"hidden": hidden, "complement": complement, "inner_weight": inner_weight, "select_weight": select_weight, "step_weight": step_weight, "step_bias": step_bias, "decay_rate": decay_rate, "skip_gain": skip_gain, "cotangent": cotangent, "complement_cotangent": complement_cotangent}


highest = lax.Precision.HIGHEST

def summary(values, write_keys, step_sizes, decay_rate):
    cumulative = jnp.cumsum(-step_sizes * decay_rate[None, :], axis=0)
    tail_weights = jnp.exp(cumulative[-1][None, :] - cumulative) * step_sizes
    state_out = jnp.einsum('sh,shp,sn->hpn', tail_weights, values, write_keys, precision=highest)
    return (state_out, cumulative[-1])

def response(values, write_keys, read_keys, step_sizes, decay_rate, state_in):
    cumulative = jnp.cumsum(-step_sizes * decay_rate[None, :], axis=0)
    length = values.shape[0]
    causal = lax.broadcasted_iota(jnp.int32, (length, length), 0) >= lax.broadcasted_iota(jnp.int32, (length, length), 1)
    cum_heads = cumulative.T
    log_gaps = cum_heads[:, :, None] - cum_heads[:, None, :]
    decays = jnp.exp(jnp.where(causal[None, :, :], log_gaps, -1e+30))
    scores = jnp.dot(read_keys, write_keys.T, precision=highest)
    weights = decays * scores[None, :, :] * step_sizes.T[:, None, :]
    within = jnp.einsum('hts,shp->thp', weights, values, precision=highest)
    carried = jnp.exp(cumulative)[:, :, None] * jnp.einsum('tn,hpn->thp', read_keys, state_in, precision=highest)
    return within + carried

def one_direction(values, write_keys, read_keys, step_sizes, decay_rate):
    blocks = values.shape[0] // RD
    block_data = (values.reshape(blocks, RD, HEADS, HEAD_DIM), write_keys.reshape(blocks, RD, STATE), read_keys.reshape(blocks, RD, STATE), step_sizes.reshape(blocks, RD, HEADS))

    def advance(state_now, piece):
        output = response(piece[0], piece[1], piece[2], piece[3], decay_rate, state_now)
        state_part, total = summary(piece[0], piece[1], piece[3], decay_rate)
        return (jnp.exp(total)[:, None, None] * state_now + state_part, output)
    initial = jnp.zeros((HEADS, HEAD_DIM, STATE), jnp.float32)
    _, outputs = lax.scan(advance, initial, block_data)
    return outputs.reshape(values.shape)

def mixer_core(values, write_keys, read_keys, raw_steps, decay_rate, step_bias, skip_gain):
    step_sizes = jax.nn.softplus(raw_steps + step_bias[None, :])
    forward_out = one_direction(values, write_keys, read_keys, step_sizes, decay_rate)
    backward_out = jnp.flip(one_direction(jnp.flip(values, 0), jnp.flip(write_keys, 0), jnp.flip(read_keys, 0), jnp.flip(step_sizes, 0), decay_rate), 0)
    return forward_out + backward_out + skip_gain[None, :, None] * values

def strand(source, grad_out, inner_weight, select_weight, step_weight, step_bias, decay_rate, skip_gain):
    values = jnp.dot(source, inner_weight, preferred_element_type=jnp.float32).astype(jnp.bfloat16)
    keys = jnp.dot(source, select_weight, preferred_element_type=jnp.float32).astype(jnp.bfloat16)
    raw_steps = jnp.dot(source, step_weight, preferred_element_type=jnp.float32)
    length = source.shape[0]

    def run(value_in, write_in, read_in, raw_in):
        result = mixer_core(value_in.reshape(length, HEADS, HEAD_DIM), write_in, read_in, raw_in, decay_rate, step_bias, skip_gain)
        return result.reshape(length, HEADS * HEAD_DIM)
    output, pullback = jax.vjp(run, values.astype(jnp.float32), keys[:, :STATE].astype(jnp.float32), keys[:, STATE:].astype(jnp.float32), raw_steps)
    d_values, d_write, d_read, d_raw = pullback(grad_out.astype(jnp.float32))
    grad_term = jnp.dot(d_values.astype(jnp.bfloat16), inner_weight.T, preferred_element_type=jnp.float32)
    grad_term = grad_term + jnp.dot(jnp.concatenate([d_write, d_read], axis=1), select_weight.astype(jnp.float32).T, precision=highest)
    grad_term = grad_term + jnp.dot(d_raw, step_weight.astype(jnp.float32).T, precision=highest)
    return (output.astype(jnp.bfloat16), grad_term)

def reference(hidden, complement, inner_weight, select_weight, step_weight, step_bias, decay_rate, skip_gain, cotangent, complement_cotangent):
    mixed, grad_term = strand(hidden, cotangent, inner_weight, select_weight, step_weight, step_bias, decay_rate, skip_gain)
    source = jnp.flip(jnp.flip(complement, 1), 0)
    other_out, other_term = strand(source, jnp.flip(complement_cotangent, 0), inner_weight, select_weight, step_weight, step_bias, decay_rate, skip_gain)
    mixed_complement = jnp.flip(other_out, 0)
    grad_hidden = grad_term.astype(jnp.bfloat16)
    grad_complement = jnp.flip(jnp.flip(other_term, 0), 1).astype(jnp.bfloat16)
    return (mixed, mixed_complement, grad_hidden, grad_complement)
```

```python
import functools

import jax
import jax.numpy as jnp
from jax import lax
from jax.experimental import pallas as pl
from jax.experimental.pallas import tpu as pltpu
from jax.sharding import PartitionSpec as P

F32 = jnp.float32
BF16 = jnp.bfloat16
HIGHEST = lax.Precision.HIGHEST
HEAD = 64
STATE = 128
ROWS = 128
FLIP = 256
LANES = 128


def dot(a, b, ca=1, cb=0, precision=None):
    return lax.dot_general(
        a, b, (((ca,), (cb,)), ((), ())), precision=precision, preferred_element_type=F32
    )


def split(a):
    high = a.astype(BF16)
    return high, (a - high.astype(F32)).astype(BF16)


def dot_left(a, b, ca=1, cb=0):
    high, low = split(a)
    return dot(high, b, ca, cb) + dot(low, b, ca, cb)


def dot_right(a, b, ca=1, cb=0):
    high, low = split(b)
    return dot(a, high, ca, cb) + dot(a, low, ca, cb)


def dot_both(a, b, ca=1, cb=0):
    a_high, a_low = split(a)
    b_high, b_low = split(b)
    return dot(a_high, b_high, ca, cb) + (dot(a_high, b_low, ca, cb) + dot(a_low, b_high, ca, cb))


def iota(shape, dim):
    return lax.broadcasted_iota(jnp.int32, shape, dim)


def where01(mask, dtype=F32):
    return jnp.where(mask, 1.0, 0.0).astype(dtype)


def anti_identity():
    return where01(iota((FLIP, FLIP), 0) + iota((FLIP, FLIP), 1) == FLIP - 1, BF16)


def spread_matrix(channels):
    lanes = iota((LANES, channels), 1)
    row = iota((LANES, channels), 0) * HEAD
    return where01((lanes >= row) & (lanes < row + HEAD))


def decay_parts(dt, rate):
    log_decay = -dt * rate
    strict = where01(iota((ROWS, ROWS), 0) > iota((ROWS, ROWS), 1))
    before = dot(strict, log_decay, precision=HIGHEST)
    upto = before + log_decay
    total = upto[ROWS - 1 : ROWS, :]
    return log_decay, before, upto, total


def project_kernel(
    hidden, complement, inner, select, step, params, cot, ccot, send, values, keys, dts, sigs, source, step_wide
):
    channels = inner.shape[1]
    heads = channels // HEAD
    bias, rate = params[0:1, :], params[1:2, :]
    depth = hidden.shape[1]
    blocks = depth // FLIP
    source[:ROWS, :] = hidden[...]
    anti = anti_identity()
    for b in range(blocks):
        block = complement[:, (blocks - 1 - b) * FLIP : (blocks - b) * FLIP]
        source[ROWS:, b * FLIP : (b + 1) * FLIP] = dot(block, anti).astype(BF16)
    src = source[...]
    v_all = dot(src, inner[...]).astype(BF16)
    k_all = dot(src, select[...]).astype(BF16)
    step_wide[...] = jnp.zeros_like(step_wide)
    step_wide[:, :heads] = step[...]
    raw = dot(src, step_wide[...]) + bias
    small = jnp.exp(-jnp.abs(raw))
    one_more = 1.0 + small
    tail = jnp.where(
        one_more == 1.0, small, jnp.log(one_more) * (small / jnp.where(one_more == 1.0, 1.0, one_more - 1.0))
    )
    dt_all = jnp.maximum(raw, 0.0) + tail
    values[...] = v_all
    keys[...] = k_all
    dts[...] = dt_all
    sigs[...] = jnp.where(raw >= 0.0, 1.0, small) / one_more
    spread = spread_matrix(channels)
    ones = jnp.ones((ROWS, STATE), F32)
    for s in range(2):
        rows = slice(s * ROWS, (s + 1) * ROWS)
        dt = dt_all[rows]
        log_decay, before, upto, total = decay_parts(dt, rate)
        x = v_all[rows].astype(F32)
        g = (cot if s == 0 else ccot)[...].astype(F32)
        write, read = k_all[rows, :STATE], k_all[rows, STATE:]
        widen = lambda w: dot(w, spread, precision=HIGHEST)
        pieces = (
            (0, 0, widen(jnp.exp(total - upto) * dt) * x, write),
            (0, HEAD, widen(jnp.exp(total - before)) * g, read),
            (1, 0, widen(jnp.exp(before) * dt) * x, write),
            (1, HEAD, widen(jnp.exp(upto)) * g, read),
        )
        for way, at, left, right in pieces:
            state = dot_left(left, right, 0, 0)
            first = (way * 2 + s) * heads
            send[first : first + heads, at : at + HEAD, :] = state.reshape(heads, HEAD, STATE)
        decay = jnp.exp(dot(log_decay, ones, 0, 0, precision=HIGHEST))
        for way in range(2):
            for h in range(heads):
                send[(way * 2 + s) * heads + h, 2 * HEAD :, :] = jnp.broadcast_to(decay[h : h + 1], (8, STATE))


def scan_kernel(shards, arrived, back):
    mine = arrived.shape[0] // shards
    me = lax.axis_index("seq")
    for j in range(mine):
        down = (me * mine + j) // (shards * mine // 2)

        def one(lap, state):
            c = lap + down * (shards - 1 - 2 * lap)
            at = c * mine + j
            back[at] = state.reshape(2 * HEAD, STATE)
            part = arrived[at]
            decay = part[2 * HEAD :]
            return state * decay[None] + part[: 2 * HEAD].reshape(2 * HEAD // 8, 8, STATE)

        lax.fori_loop(0, shards, one, jnp.zeros((2 * HEAD // 8, 8, STATE), F32))


def finish_kernel(
    entry,
    values,
    keys,
    dts,
    sigs,
    inner,
    select,
    step,
    params,
    cot,
    ccot,
    mixed,
    cmixed,
    term,
    d_val,
    d_key,
    d_raw,
    step_wide,
):
    channels = values.shape[1]
    heads = channels // HEAD
    rate, skip = params[1:2, :], params[2:3, :]
    step_wide[...] = jnp.zeros_like(step_wide)
    step_wide[:, :heads] = step[...]
    spread = spread_matrix(channels)
    row_id, col_id = iota((ROWS, ROWS), 0), iota((ROWS, ROWS), 1)
    diagonal, lower, upper = row_id == col_id, row_id > col_id, row_id < col_id
    eye = where01(diagonal)
    twice = jnp.where(diagonal, 2.0, 1.0)
    lane_first = where01(iota((1, 2 * HEAD), 1) < HEAD, BF16)
    lane_second = where01(iota((1, 2 * HEAD), 1) >= HEAD, BF16)
    head_lane = iota((ROWS, LANES), 1)
    head_row = iota((heads, ROWS), 0)
    widen = lambda w: dot(w, spread, precision=HIGHEST)
    narrow = lambda w: dot(w, spread, 1, 1, precision=HIGHEST)
    skip_wide = widen(skip)
    for s in range(2):
        rows = slice(s * ROWS, (s + 1) * ROWS)
        dt = dts[rows, :]
        log_decay, before, upto, total = decay_parts(dt, rate)
        dt_t = dot(dt, eye, 0, 0, precision=HIGHEST)
        before_t = dot(log_decay, where01(upper), 0, 0, precision=HIGHEST)
        upto_t = before_t + dot(log_decay, eye, 0, 0, precision=HIGHEST)
        x_b, g_b = values[rows, :], (cot if s == 0 else ccot)[...]
        x, g = x_b.astype(F32), g_b.astype(F32)
        write, read = keys[rows, :STATE], keys[rows, STATE:]
        u_fwd, u_bwd = widen(jnp.exp(total - upto)), widen(jnp.exp(before))
        w_fwd, w_bwd = widen(jnp.exp(upto)), widen(jnp.exp(total - before))
        dt_wide = widen(dt)
        state = lambda way, at: entry[
            (way * 2 + s) * heads : (way * 2 + s + 1) * heads, at : at + HEAD, :
        ].reshape(heads * HEAD, STATE)
        h_in, m_in, k_in, l_in = state(0, 0), state(0, HEAD), state(1, 0), state(1, HEAD)
        y_fwd = w_fwd * dot_right(read, h_in, 1, 1)
        y_bwd = w_bwd * dot_right(read, k_in, 1, 1)
        x_l = u_fwd * dot_right(write, l_in, 1, 1)
        x_m = u_bwd * dot_right(write, m_in, 1, 1)
        d_read = dot_both(w_fwd * g, h_in) + dot_both(w_bwd * g, k_in)
        d_write = dot_both(u_fwd * dt_wide * x, l_in) + dot_both(u_bwd * dt_wide * x, m_in)
        r_fwd, r_bwd = narrow(g * y_fwd), narrow(g * y_bwd)
        q_fwd, q_bwd = narrow(x * x_l), narrow(x * x_m)
        both = dot(spread, l_in * h_in + m_in * k_in, precision=HIGHEST)
        both = dot(jnp.ones((8, STATE), F32), both, 1, 1, precision=HIGHEST)[0:1]
        scores = dot(read, write, 1, 1)
        d_scores = jnp.zeros((ROWS, ROWS), F32)
        by_row = jnp.zeros((ROWS, LANES), F32)
        by_row_up = jnp.zeros((ROWS, LANES), F32)
        direct_t = jnp.zeros((heads, ROWS), F32)
        low_t = jnp.zeros((heads, ROWS), F32)
        up_t = jnp.zeros((heads, ROWS), F32)
        for pair in range(heads // 2):
            lanes = slice(pair * 2 * HEAD, (pair + 1) * 2 * HEAD)
            x_pair, g_pair = x_b[:, lanes], g_b[:, lanes]
            y_pair = jnp.zeros((ROWS, 2 * HEAD), F32)
            d_pair = jnp.zeros((ROWS, 2 * HEAD), F32)
            for half, lane_mask in ((0, lane_first), (1, lane_second)):
                h = pair * 2 + half
                x_h, g_h = x_pair * lane_mask, g_pair * lane_mask
                gap = jnp.where(
                    upper,
                    before_t[h : h + 1, :] - before[:, h : h + 1],
                    upto[:, h : h + 1] - upto_t[h : h + 1, :],
                )
                decay = jnp.exp(jnp.minimum(gap, 0.0)) * twice
                dt_row = dt_t[h : h + 1, :]
                scaled = scores * decay
                weights = scaled * dt_row
                w_high, w_low = split(weights)
                y_pair = y_pair + (dot(w_high, x_h) + dot(w_low, x_h))
                d_pair = d_pair + (dot(w_high, g_h, 0, 0) + dot(w_low, g_h, 0, 0))
                outer = dot(g_h, x_pair, 1, 1)
                grads = outer * scaled
                d_scores = d_scores + outer * (decay * dt_row)
                q = grads * dt_row
                q_low, q_up = jnp.where(lower, q, 0.0), jnp.where(upper, q, 0.0)
                by_row = jnp.where(head_lane == h, jnp.sum(q_low, 1, keepdims=True), by_row)
                by_row_up = jnp.where(head_lane == h, jnp.sum(q_up, 1, keepdims=True), by_row_up)
                direct_t = jnp.where(head_row == h, jnp.sum(grads, 0, keepdims=True), direct_t)
                low_t = jnp.where(head_row == h, jnp.sum(q_low, 0, keepdims=True), low_t)
                up_t = jnp.where(head_row == h, jnp.sum(q_up, 0, keepdims=True), up_t)
            out = y_pair + y_fwd[:, lanes] + y_bwd[:, lanes] + skip_wide[:, lanes] * x[:, lanes]
            (mixed if s == 0 else cmixed)[:, lanes] = out.astype(BF16)
            grad = d_pair + dt_wide[:, lanes] * (x_l[:, lanes] + x_m[:, lanes])
            grad = grad + skip_wide[:, lanes] * g[:, lanes]
            d_val[rows, lanes] = grad.astype(BF16)
        stacked = (direct_t, low_t, up_t, jnp.zeros((ROWS - 3 * heads, ROWS), F32))
        turned = jnp.transpose(jnp.concatenate(stacked, 0))
        picked = lambda at: jnp.where(head_lane < heads, pltpu.roll(turned, LANES - at, 1) if at else turned, 0.0)
        d_dt = picked(0) + q_fwd + q_bwd
        d_upto = by_row - picked(heads) + r_fwd - dt * q_fwd
        d_before = picked(2 * heads) - by_row_up - r_bwd + dt * q_bwd
        d_total = jnp.sum(r_bwd + dt * q_fwd, 0, keepdims=True) + jnp.exp(total) * both
        from_here = where01(row_id <= col_id)
        d_log = dot(from_here, d_upto, precision=HIGHEST) + dot(where01(upper), d_before, precision=HIGHEST)
        d_log = d_log + d_total
        d_raw[rows, :] = (d_dt - rate * d_log) * sigs[rows, :]
        d_key[rows, :STATE] = d_write + dot_left(d_scores, read, 0, 0)
        d_key[rows, STATE:] = d_read + dot_left(d_scores, write)
    chunks = term.shape[0]
    width = term.shape[2]
    val = d_val[...]
    key_high, key_low = split(d_key[...])
    raw_high, raw_low = split(d_raw[...])
    for j in range(chunks):
        cols = slice(j * width, (j + 1) * width)
        part = dot(val, inner[cols, :], 1, 1)
        sel, stp = select[cols, :], step_wide[cols, :]
        part = part + (dot(key_high, sel, 1, 1) + dot(key_low, sel, 1, 1))
        part = part + (dot(raw_high, stp, 1, 1) + dot(raw_low, stp, 1, 1))
        term[j, :ROWS, :] = part[:ROWS]
        term[chunks - 1 - j, ROWS:, :] = part[ROWS:]


def combine_kernel(shares, first, second):
    total = shares[0]
    for j in range(1, shares.shape[0]):
        total = total + shares[j]
    total = total.astype(BF16)
    first[...] = total[:ROWS]
    anti = anti_identity()
    blocks = total.shape[1] // FLIP
    for b in range(blocks):
        block = total[ROWS:, (blocks - 1 - b) * FLIP : (blocks - b) * FLIP]
        second[:, b * FLIP : (b + 1) * FLIP] = dot(block, anti).astype(BF16)


def call(kernel, outs, args, scratch=()):
    whole = pl.BlockSpec(memory_space=pltpu.VMEM)
    return pl.pallas_call(
        kernel,
        out_shape=[jax.ShapeDtypeStruct(shape, dtype) for shape, dtype in outs],
        in_specs=[whole] * len(args),
        out_specs=[whole] * len(outs),
        scratch_shapes=[pltpu.VMEM(shape, dtype) for shape, dtype in scratch],
        compiler_params=pltpu.CompilerParams(vmem_limit_bytes=48 << 20),
    )(*args)


def local(hidden, complement, inner, select, step, bias, rate, skip, cot, ccot):
    shards, ranks = lax.axis_size("seq"), lax.axis_size("chan")
    heads = bias.shape[0]
    depth = hidden.shape[1]
    channels = heads * HEAD
    params = jnp.pad(jnp.stack([bias, rate, skip]), ((0, 5), (0, LANES - heads)))
    send, values, keys, dts, sigs = call(
        project_kernel,
        [
            ((4 * heads, 2 * HEAD + 8, STATE), F32),
            ((2 * ROWS, channels), BF16),
            ((2 * ROWS, 2 * STATE), BF16),
            ((2 * ROWS, LANES), F32),
            ((2 * ROWS, LANES), F32),
        ],
        (hidden, complement, inner, select, step, params, cot, ccot),
        [((2 * ROWS, depth), BF16), ((depth, LANES), BF16)],
    )
    arrived = lax.all_to_all(send, "seq", 0, 0, tiled=True)
    (back,) = call(
        functools.partial(scan_kernel, shards), [((4 * heads, 2 * HEAD, STATE), F32)], (arrived,)
    )
    entry = lax.all_to_all(back, "seq", 0, 0, tiled=True)
    mixed, cmixed, term = call(
        finish_kernel,
        [
            ((ROWS, channels), BF16),
            ((ROWS, channels), BF16),
            ((ranks, 2 * ROWS, depth // ranks), F32),
        ],
        (entry, values, keys, dts, sigs, inner, select, step, params, cot, ccot),
        [
            ((2 * ROWS, channels), BF16),
            ((2 * ROWS, 2 * STATE), F32),
            ((2 * ROWS, LANES), F32),
            ((depth, LANES), BF16),
        ],
    )
    shares = lax.all_to_all(term, "chan", 0, 0, tiled=True)
    first, second = call(combine_kernel, [((ROWS, depth // ranks), BF16)] * 2, (shares,))
    return mixed, cmixed, first, second


def solution(mesh):
    rows = P(("dp", "seq"), None)
    tiles = P(("dp", "seq"), "chan")
    in_specs = (rows, rows, P(None, "chan"), P(), P(None, "chan"), P("chan"), P("chan"), P("chan"), tiles, tiles)
    return jax.shard_map(
        local, mesh=mesh, in_specs=in_specs, out_specs=(tiles,) * 4, check_vma=False
    )
```

```python
import functools

import jax
import jax.numpy as jnp
from jax import lax
from jax.experimental import pallas as pl
from jax.experimental.pallas import tpu as pltpu
from jax.sharding import PartitionSpec as P

F32 = jnp.float32
BF16 = jnp.bfloat16
HIGHEST = lax.Precision.HIGHEST
HEAD = 64
STATE = 128
ROWS = 128
FLIP = 256
LANES = 128


def dot(a, b, ca=1, cb=0, precision=None):
    return lax.dot_general(
        a, b, (((ca,), (cb,)), ((), ())), precision=precision, preferred_element_type=F32
    )


def split(a):
    high = a.astype(BF16)
    return high, (a - high.astype(F32)).astype(BF16)


def dot_left(a, b, ca=1, cb=0):
    high, low = split(a)
    return dot(high, b, ca, cb) + dot(low, b, ca, cb)


def dot_right(a, b, ca=1, cb=0):
    high, low = split(b)
    return dot(a, high, ca, cb) + dot(a, low, ca, cb)


def dot_both(a, b, ca=1, cb=0):
    a_high, a_low = split(a)
    b_high, b_low = split(b)
    return dot(a_high, b_high, ca, cb) + (dot(a_high, b_low, ca, cb) + dot(a_low, b_high, ca, cb))


def iota(shape, dim):
    return lax.broadcasted_iota(jnp.int32, shape, dim)


def where01(mask, dtype=F32):
    return jnp.where(mask, 1.0, 0.0).astype(dtype)


def anti_identity():
    return where01(iota((FLIP, FLIP), 0) + iota((FLIP, FLIP), 1) == FLIP - 1, BF16)


def spread_matrix(channels):
    lanes = iota((LANES, channels), 1)
    row = iota((LANES, channels), 0) * HEAD
    return where01((lanes >= row) & (lanes < row + HEAD))


def decay_parts(dt, rate):
    log_decay = -dt * rate
    strict = where01(iota((ROWS, ROWS), 0) > iota((ROWS, ROWS), 1))
    before = dot(strict, log_decay, precision=HIGHEST)
    upto = before + log_decay
    total = upto[ROWS - 1 : ROWS, :]
    return log_decay, before, upto, total


def project_kernel(
    hidden_hbm,
    complement_hbm,
    inner_hbm,
    select_hbm,
    cot_hbm,
    ccot_hbm,
    step,
    params,
    send,
    values,
    keys,
    dts,
    sigs,
    source,
    step_wide,
    complement,
    inner,
    select,
    cot,
    ccot,
    sems,
):
    channels = inner.shape[1]
    heads = channels // HEAD
    bias, rate = params[0:1, :], params[1:2, :]
    fetches = [
        pltpu.make_async_copy(here, there, sems.at[i])
        for i, (here, there) in enumerate(
            (
                (complement_hbm, complement),
                (hidden_hbm, source.at[:ROWS]),
                (select_hbm, select),
                (inner_hbm, inner),
                (cot_hbm, cot),
                (ccot_hbm, ccot),
            )
        )
    ]
    for fetch in fetches:
        fetch.start()
    depth = complement.shape[1]
    blocks = depth // FLIP
    anti = anti_identity()
    fetches[0].wait()
    for b in range(blocks):
        block = complement[:, (blocks - 1 - b) * FLIP : (blocks - b) * FLIP]
        source[ROWS:, b * FLIP : (b + 1) * FLIP] = dot(block, anti).astype(BF16)
    step_wide[...] = jnp.zeros_like(step_wide)
    step_wide[:heads, :] = step[...]
    fetches[1].wait()
    src = source[...]
    raw = dot(src, step_wide[...], 1, 1) + bias
    fetches[2].wait()
    k_all = dot(src, select[...]).astype(BF16)
    fetches[3].wait()
    v_all = dot(src, inner[...]).astype(BF16)
    fetches[4].wait()
    fetches[5].wait()
    small = jnp.exp(-jnp.abs(raw))
    one_more = 1.0 + small
    tail = jnp.where(
        one_more == 1.0, small, jnp.log(one_more) * (small / jnp.where(one_more == 1.0, 1.0, one_more - 1.0))
    )
    dt_all = jnp.maximum(raw, 0.0) + tail
    values[...] = v_all
    keys[...] = k_all
    dts[...] = dt_all
    sigs[...] = jnp.where(raw >= 0.0, 1.0, small) / one_more
    spread = spread_matrix(channels)
    ones = jnp.ones((ROWS, STATE), F32)
    for s in range(2):
        rows = slice(s * ROWS, (s + 1) * ROWS)
        dt = dt_all[rows]
        log_decay, before, upto, total = decay_parts(dt, rate)
        x = v_all[rows].astype(F32)
        g = (cot if s == 0 else ccot)[...].astype(F32)
        write, read = k_all[rows, :STATE], k_all[rows, STATE:]
        widen = lambda w: dot(w, spread, precision=HIGHEST)
        pieces = (
            (0, 0, widen(jnp.exp(total - upto) * dt) * x, write),
            (0, HEAD, widen(jnp.exp(total - before)) * g, read),
            (1, 0, widen(jnp.exp(before) * dt) * x, write),
            (1, HEAD, widen(jnp.exp(upto)) * g, read),
        )
        for way, at, left, right in pieces:
            state = dot_left(left, right, 0, 0)
            first = (way * 2 + s) * heads
            send[first : first + heads, at : at + HEAD, :] = state.reshape(heads, HEAD, STATE)
        decay = jnp.exp(dot(log_decay, ones, 0, 0, precision=HIGHEST))
        for way in range(2):
            for h in range(heads):
                send[(way * 2 + s) * heads + h, 2 * HEAD :, :] = jnp.broadcast_to(decay[h : h + 1], (8, STATE))


def scan_kernel(shards, arrived, back):
    mine = arrived.shape[0] // shards
    me = lax.axis_index("seq")
    for j in range(mine):
        down = (me * mine + j) // (shards * mine // 2)

        def one(lap, state):
            c = lap + down * (shards - 1 - 2 * lap)
            at = c * mine + j
            back[at] = state.reshape(2 * HEAD, STATE)
            part = arrived[at]
            decay = part[2 * HEAD :]
            return state * decay[None] + part[: 2 * HEAD].reshape(2 * HEAD // 8, 8, STATE)

        lax.fori_loop(0, shards, one, jnp.zeros((2 * HEAD // 8, 8, STATE), F32))


def finish_kernel(
    entry,
    values,
    keys,
    dts,
    sigs,
    params,
    cot,
    ccot,
    mixed,
    cmixed,
    d_val,
    d_key_high,
    d_key_low,
    d_raw_high,
    d_raw_low,
):
    channels = values.shape[1]
    heads = channels // HEAD
    rate, skip = params[1:2, :], params[2:3, :]
    spread = spread_matrix(channels)
    row_id, col_id = iota((ROWS, ROWS), 0), iota((ROWS, ROWS), 1)
    diagonal, lower, upper = row_id == col_id, row_id > col_id, row_id < col_id
    eye = where01(diagonal)
    twice = jnp.where(diagonal, 2.0, 1.0)
    lane_first = where01(iota((1, 2 * HEAD), 1) < HEAD, BF16)
    lane_second = where01(iota((1, 2 * HEAD), 1) >= HEAD, BF16)
    head_lane = iota((ROWS, LANES), 1)
    head_row = iota((heads, ROWS), 0)
    widen = lambda w: dot(w, spread, precision=HIGHEST)
    narrow = lambda w: dot(w, spread, 1, 1, precision=HIGHEST)
    skip_wide = widen(skip)
    for s in range(2):
        rows = slice(s * ROWS, (s + 1) * ROWS)
        dt = dts[rows, :]
        log_decay, before, upto, total = decay_parts(dt, rate)
        dt_t = dot(dt, eye, 0, 0, precision=HIGHEST)
        before_t = dot(log_decay, where01(upper), 0, 0, precision=HIGHEST)
        upto_t = before_t + dot(log_decay, eye, 0, 0, precision=HIGHEST)
        x_b, g_b = values[rows, :], (cot if s == 0 else ccot)[...]
        x, g = x_b.astype(F32), g_b.astype(F32)
        write, read = keys[rows, :STATE], keys[rows, STATE:]
        u_fwd, u_bwd = widen(jnp.exp(total - upto)), widen(jnp.exp(before))
        w_fwd, w_bwd = widen(jnp.exp(upto)), widen(jnp.exp(total - before))
        dt_wide = widen(dt)
        state = lambda way, at: entry[
            (way * 2 + s) * heads : (way * 2 + s + 1) * heads, at : at + HEAD, :
        ].reshape(heads * HEAD, STATE)
        h_in, m_in, k_in, l_in = state(0, 0), state(0, HEAD), state(1, 0), state(1, HEAD)
        y_fwd = w_fwd * dot_right(read, h_in, 1, 1)
        y_bwd = w_bwd * dot_right(read, k_in, 1, 1)
        x_l = u_fwd * dot_right(write, l_in, 1, 1)
        x_m = u_bwd * dot_right(write, m_in, 1, 1)
        d_read = dot_both(w_fwd * g, h_in) + dot_both(w_bwd * g, k_in)
        d_write = dot_both(u_fwd * dt_wide * x, l_in) + dot_both(u_bwd * dt_wide * x, m_in)
        r_fwd, r_bwd = narrow(g * y_fwd), narrow(g * y_bwd)
        q_fwd, q_bwd = narrow(x * x_l), narrow(x * x_m)
        both = dot(spread, l_in * h_in + m_in * k_in, precision=HIGHEST)
        both = dot(jnp.ones((8, STATE), F32), both, 1, 1, precision=HIGHEST)[0:1]
        scores = dot(read, write, 1, 1)
        d_scores = jnp.zeros((ROWS, ROWS), F32)
        by_row = jnp.zeros((ROWS, LANES), F32)
        by_row_up = jnp.zeros((ROWS, LANES), F32)
        direct_t = jnp.zeros((heads, ROWS), F32)
        low_t = jnp.zeros((heads, ROWS), F32)
        up_t = jnp.zeros((heads, ROWS), F32)
        for pair in range(heads // 2):
            lanes = slice(pair * 2 * HEAD, (pair + 1) * 2 * HEAD)
            x_pair, g_pair = x_b[:, lanes], g_b[:, lanes]
            y_pair = jnp.zeros((ROWS, 2 * HEAD), F32)
            d_pair = jnp.zeros((ROWS, 2 * HEAD), F32)
            for half, lane_mask in ((0, lane_first), (1, lane_second)):
                h = pair * 2 + half
                x_h, g_h = x_pair * lane_mask, g_pair * lane_mask
                gap = jnp.where(
                    upper,
                    before_t[h : h + 1, :] - before[:, h : h + 1],
                    upto[:, h : h + 1] - upto_t[h : h + 1, :],
                )
                decay = jnp.exp(jnp.minimum(gap, 0.0)) * twice
                dt_row = dt_t[h : h + 1, :]
                scaled = scores * decay
                weights = scaled * dt_row
                w_high, w_low = split(weights)
                y_pair = y_pair + (dot(w_high, x_h) + dot(w_low, x_h))
                d_pair = d_pair + (dot(w_high, g_h, 0, 0) + dot(w_low, g_h, 0, 0))
                outer = dot(g_h, x_pair, 1, 1)
                grads = outer * scaled
                d_scores = d_scores + outer * (decay * dt_row)
                q = grads * dt_row
                q_low, q_up = jnp.where(lower, q, 0.0), jnp.where(upper, q, 0.0)
                by_row = jnp.where(head_lane == h, jnp.sum(q_low, 1, keepdims=True), by_row)
                by_row_up = jnp.where(head_lane == h, jnp.sum(q_up, 1, keepdims=True), by_row_up)
                direct_t = jnp.where(head_row == h, jnp.sum(grads, 0, keepdims=True), direct_t)
                low_t = jnp.where(head_row == h, jnp.sum(q_low, 0, keepdims=True), low_t)
                up_t = jnp.where(head_row == h, jnp.sum(q_up, 0, keepdims=True), up_t)
            out = y_pair + y_fwd[:, lanes] + y_bwd[:, lanes] + skip_wide[:, lanes] * x[:, lanes]
            (mixed if s == 0 else cmixed)[:, lanes] = out.astype(BF16)
            grad = d_pair + dt_wide[:, lanes] * (x_l[:, lanes] + x_m[:, lanes])
            grad = grad + skip_wide[:, lanes] * g[:, lanes]
            d_val[rows, lanes] = grad.astype(BF16)
        stacked = (direct_t, low_t, up_t, jnp.zeros((ROWS - 3 * heads, ROWS), F32))
        turned = jnp.transpose(jnp.concatenate(stacked, 0))
        picked = lambda at: jnp.where(head_lane < heads, pltpu.roll(turned, LANES - at, 1) if at else turned, 0.0)
        d_dt = picked(0) + q_fwd + q_bwd
        d_upto = by_row - picked(heads) + r_fwd - dt * q_fwd
        d_before = picked(2 * heads) - by_row_up - r_bwd + dt * q_bwd
        d_total = jnp.sum(r_bwd + dt * q_fwd, 0, keepdims=True) + jnp.exp(total) * both
        from_here = where01(row_id <= col_id)
        d_log = dot(from_here, d_upto, precision=HIGHEST) + dot(where01(upper), d_before, precision=HIGHEST)
        d_log = d_log + d_total
        d_raw_high[rows, :], d_raw_low[rows, :] = split((d_dt - rate * d_log) * sigs[rows, :])
        d_write = d_write + dot_left(d_scores, read, 0, 0)
        d_read = d_read + dot_left(d_scores, write)
        d_key_high[rows, :STATE], d_key_low[rows, :STATE] = split(d_write)
        d_key_high[rows, STATE:], d_key_low[rows, STATE:] = split(d_read)


def reduce_kernel(
    ranks,
    d_val,
    d_key_high,
    d_key_low,
    d_raw_high,
    d_raw_low,
    inner,
    select,
    step,
    first,
    second,
    step_wide,
    term,
    arrived,
    send_sems,
    recv_sems,
):
    me = lax.axis_index("chan")
    width = term.shape[2]
    heads = step.shape[0]
    barrier = pltpu.get_barrier_semaphore()
    for j in range(1, ranks):
        pl.semaphore_signal(
            barrier, inc=1, device_id={"chan": lax.rem(me + j, ranks)}, device_id_type=pl.DeviceIdType.MESH
        )
    step_wide[...] = jnp.zeros_like(step_wide)
    step_wide[:heads, :] = step[...]

    def chunk(rows, rank):
        at = pl.multiple_of(rank * width, width)
        cols = pl.ds(at, width)
        part = dot(d_val[rows, :], inner[cols, :], 1, 1)
        keys = select[cols, :]
        part = part + (dot(d_key_high[rows, :], keys, 1, 1) + dot(d_key_low[rows, :], keys, 1, 1))
        steps = step_wide[:, cols]
        return part + (dot(d_raw_high[rows, :], steps) + dot(d_raw_low[rows, :], steps))

    def share(rank):
        term[rank, :ROWS, :] = chunk(slice(0, ROWS), rank)
        term[rank, ROWS:, :] = chunk(slice(ROWS, 2 * ROWS), ranks - 1 - rank)

    def copy(j):
        peer = lax.rem(me + j, ranks)
        return pltpu.make_async_remote_copy(
            src_ref=term.at[peer],
            dst_ref=arrived.at[me],
            send_sem=send_sems.at[j],
            recv_sem=recv_sems.at[j],
            device_id={"chan": peer},
            device_id_type=pl.DeviceIdType.MESH,
        )

    share(lax.rem(me + 1, ranks))
    pl.semaphore_wait(barrier, ranks - 1)
    copy(1).start()
    for j in range(2, ranks):
        share(lax.rem(me + j, ranks))
        copy(j).start()
    share(me)
    total = term[me]
    for j in range(1, ranks):
        copy(j).wait_recv()
        total = total + arrived[lax.rem(me + ranks - j, ranks)]
    for j in range(1, ranks):
        copy(j).wait_send()
    total = total.astype(BF16)
    first[...] = total[:ROWS]
    anti = anti_identity()
    blocks = width // FLIP
    for b in range(blocks):
        block = total[ROWS:, (blocks - 1 - b) * FLIP : (blocks - b) * FLIP]
        second[:, b * FLIP : (b + 1) * FLIP] = dot(block, anti).astype(BF16)


def call(kernel, outs, args, scratch=(), far=0, **params):
    whole = pl.BlockSpec(memory_space=pltpu.VMEM)
    return pl.pallas_call(
        kernel,
        out_shape=[jax.ShapeDtypeStruct(shape, dtype) for shape, dtype in outs],
        in_specs=[pl.BlockSpec(memory_space=pltpu.HBM)] * far + [whole] * (len(args) - far),
        out_specs=[whole] * len(outs),
        scratch_shapes=list(scratch),
        compiler_params=pltpu.CompilerParams(vmem_limit_bytes=48 << 20, **params),
    )(*args)


def local(hidden, complement, inner, select, step, bias, rate, skip, cot, ccot):
    shards, ranks = lax.axis_size("seq"), lax.axis_size("chan")
    heads = bias.shape[0]
    depth = hidden.shape[1]
    channels = heads * HEAD
    params = jnp.pad(jnp.stack([bias, rate, skip]), ((0, 5), (0, LANES - heads)))
    step = step.T
    send, values, keys, dts, sigs = call(
        project_kernel,
        [
            ((4 * heads, 2 * HEAD + 8, STATE), F32),
            ((2 * ROWS, channels), BF16),
            ((2 * ROWS, 2 * STATE), BF16),
            ((2 * ROWS, LANES), F32),
            ((2 * ROWS, LANES), F32),
        ],
        (hidden, complement, inner, select, cot, ccot, step, params),
        [
            pltpu.VMEM((2 * ROWS, depth), BF16),
            pltpu.VMEM((LANES, depth), BF16),
            pltpu.VMEM((ROWS, depth), BF16),
            pltpu.VMEM(inner.shape, BF16),
            pltpu.VMEM(select.shape, BF16),
            pltpu.VMEM(cot.shape, BF16),
            pltpu.VMEM(ccot.shape, BF16),
            pltpu.SemaphoreType.DMA((6,)),
        ],
        far=6,
    )
    arrived = lax.all_to_all(send, "seq", 0, 0, tiled=True)
    (back,) = call(
        functools.partial(scan_kernel, shards), [((4 * heads, 2 * HEAD, STATE), F32)], (arrived,)
    )
    entry = lax.all_to_all(back, "seq", 0, 0, tiled=True)
    mixed, cmixed, *grads = call(
        finish_kernel,
        [
            ((ROWS, channels), BF16),
            ((ROWS, channels), BF16),
            ((2 * ROWS, channels), BF16),
            ((2 * ROWS, 2 * STATE), BF16),
            ((2 * ROWS, 2 * STATE), BF16),
            ((2 * ROWS, LANES), BF16),
            ((2 * ROWS, LANES), BF16),
        ],
        (entry, values, keys, dts, sigs, params, cot, ccot),
    )
    share = (ranks, 2 * ROWS, depth // ranks)
    first, second = call(
        functools.partial(reduce_kernel, ranks),
        [((ROWS, depth // ranks), BF16)] * 2,
        (*grads, inner, select, step),
        [
            pltpu.VMEM((LANES, depth), BF16),
            pltpu.VMEM(share, F32),
            pltpu.VMEM(share, F32),
            pltpu.SemaphoreType.DMA((ranks,)),
            pltpu.SemaphoreType.DMA((ranks,)),
        ],
        collective_id=1,
        has_side_effects=True,
    )
    return mixed, cmixed, first, second


def solution(mesh):
    rows = P(("dp", "seq"), None)
    tiles = P(("dp", "seq"), "chan")
    in_specs = (rows, rows, P(None, "chan"), P(), P(None, "chan"), P("chan"), P("chan"), P("chan"), tiles, tiles)
    return jax.shard_map(
        local, mesh=mesh, in_specs=in_specs, out_specs=(tiles,) * 4, check_vma=False
    )
```

```python
import functools

import jax
import jax.numpy as jnp
from jax import lax
from jax.experimental import pallas as pl
from jax.experimental.pallas import tpu as pltpu
from jax.sharding import PartitionSpec as P

F32 = jnp.float32
BF16 = jnp.bfloat16
HIGHEST = lax.Precision.HIGHEST
HEAD = 64
STATE = 128
ROWS = 128
FLIP = 256
LANES = 128
ROW = 4


def dot(a, b, ca=1, cb=0, precision=None):
    return lax.dot_general(
        a, b, (((ca,), (cb,)), ((), ())), precision=precision, preferred_element_type=F32
    )


def split(a):
    high = a.astype(BF16)
    return high, (a - high.astype(F32)).astype(BF16)


def dot_left(a, b, ca=1, cb=0):
    high, low = split(a)
    return dot(high, b, ca, cb) + dot(low, b, ca, cb)


def dot_right(a, b, ca=1, cb=0):
    high, low = split(b)
    return dot(a, high, ca, cb) + dot(a, low, ca, cb)


def dot_both(a, b, ca=1, cb=0):
    a_high, a_low = split(a)
    b_high, b_low = split(b)
    return dot(a_high, b_high, ca, cb) + (dot(a_high, b_low, ca, cb) + dot(a_low, b_high, ca, cb))


def iota(shape, dim):
    return lax.broadcasted_iota(jnp.int32, shape, dim)


def where01(mask, dtype=F32):
    return jnp.where(mask, 1.0, 0.0).astype(dtype)


def anti_identity():
    return where01(iota((FLIP, FLIP), 0) + iota((FLIP, FLIP), 1) == FLIP - 1, BF16)


def spread_matrix(channels):
    lanes = iota((LANES, channels), 1)
    row = iota((LANES, channels), 0) * HEAD
    return where01((lanes >= row) & (lanes < row + HEAD))


def decay_parts(dt, rate):
    log_decay = -dt * rate
    strict = where01(iota((ROWS, ROWS), 0) > iota((ROWS, ROWS), 1))
    before = dot(strict, log_decay, precision=HIGHEST)
    upto = before + log_decay
    total = upto[ROWS - 1 : ROWS, :]
    return log_decay, before, upto, total


def project_kernel(
    hidden_hbm,
    complement_hbm,
    inner_hbm,
    select_hbm,
    cot_hbm,
    ccot_hbm,
    step_hbm,
    params,
    send,
    values,
    keys,
    dts,
    sigs,
    source,
    step_wide,
    complement,
    inner,
    select,
    cot,
    ccot,
    step,
    sems,
):
    channels = inner.shape[1]
    heads = channels // HEAD
    bias, rate = params[0:1, :], params[1:2, :]
    fetches = [
        pltpu.make_async_copy(here, there, sems.at[i])
        for i, (here, there) in enumerate(
            (
                (complement_hbm, complement),
                (hidden_hbm, source.at[:ROWS]),
                (select_hbm, select),
                (inner_hbm, inner),
                (cot_hbm, cot),
                (ccot_hbm, ccot),
                (step_hbm, step),
            )
        )
    ]
    for fetch in fetches:
        fetch.start()
    depth = complement.shape[1]
    blocks = depth // FLIP
    anti = anti_identity()
    fetches[0].wait()
    for b in range(blocks):
        block = complement[:, (blocks - 1 - b) * FLIP : (blocks - b) * FLIP]
        source[ROWS:, b * FLIP : (b + 1) * FLIP] = dot(block, anti).astype(BF16)
    step_wide[...] = jnp.zeros_like(step_wide)
    fetches[6].wait()
    step_wide[:heads, :] = step[...]
    fetches[1].wait()
    src = source[...]
    raw = dot(src, step_wide[...], 1, 1) + bias
    fetches[2].wait()
    k_all = dot(src, select[...]).astype(BF16)
    fetches[3].wait()
    v_all = dot(src, inner[...]).astype(BF16)
    fetches[4].wait()
    fetches[5].wait()
    small = jnp.exp(-jnp.abs(raw))
    one_more = 1.0 + small
    tail = jnp.where(
        one_more == 1.0, small, jnp.log(one_more) * (small / jnp.where(one_more == 1.0, 1.0, one_more - 1.0))
    )
    dt_all = jnp.maximum(raw, 0.0) + tail
    values[...] = v_all
    keys[...] = k_all
    dts[...] = dt_all
    sigs[...] = jnp.where(raw >= 0.0, 1.0, small) / one_more
    spread = spread_matrix(channels)
    ones = jnp.ones((ROWS, STATE), F32)
    for s in range(2):
        rows = slice(s * ROWS, (s + 1) * ROWS)
        dt = dt_all[rows]
        log_decay, before, upto, total = decay_parts(dt, rate)
        x = v_all[rows].astype(F32)
        g = (cot if s == 0 else ccot)[...].astype(F32)
        write, read = k_all[rows, :STATE], k_all[rows, STATE:]
        widen = lambda w: dot(w, spread, precision=HIGHEST)
        second = channels + 8 * heads
        pieces = (
            (0, 0, widen(jnp.exp(total - upto) * dt) * x, write),
            (0, second, widen(jnp.exp(total - before)) * g, read),
            (1, 0, widen(jnp.exp(before) * dt) * x, write),
            (1, second, widen(jnp.exp(upto)) * g, read),
        )
        for way, at, left, right in pieces:
            state = dot_left(left, right, 0, 0)
            send[way * 2 + s, at : at + channels, :] = state
        decay = jnp.exp(dot(log_decay, ones, 0, 0, precision=HIGHEST))
        for way in range(2):
            for h in range(heads):
                at = channels + 8 * h
                send[way * 2 + s, at : at + 8, :] = jnp.broadcast_to(decay[h : h + 1], (8, STATE))


def exchange_kernel(
    layers,
    heads,
    send,
    entry,
    rows_in,
    sums_a,
    sums_b,
    layers_a,
    layers_b,
    scanned_a,
    scanned_b,
    before_a,
    before_b,
    members_a,
    members_b,
    gather_out,
    gather_in,
    up_out,
    up_in,
    back_out,
    back_in,
    spread_out,
    spread_in,
):
    me = lax.axis_index("seq")
    layer, member = me // ROW, lax.rem(me, ROW)
    down = member // 2
    each = heads // layers
    channels = heads * HEAD
    side = lambda j: layer * ROW + lax.rem(member + j, ROW)
    over = lambda j: lax.rem(layer + j, layers) * ROW + member
    place = {"device_id_type": pl.DeviceIdType.MESH}
    barrier = pltpu.get_barrier_semaphore()
    for j in range(1, ROW):
        pl.semaphore_signal(barrier, inc=1, device_id={"seq": side(j)}, **place)
    for j in range(1, layers):
        pl.semaphore_signal(barrier, inc=1, device_id={"seq": over(j)}, **place)
    pl.semaphore_wait(barrier, ROW + layers - 2)
    spans = (pl.ds(0, channels + 8 * heads), pl.ds(channels + 8 * heads, channels))

    def gather(half, j):
        return pltpu.make_async_remote_copy(
            src_ref=send.at[lax.rem(member + j, ROW), spans[half]],
            dst_ref=rows_in.at[member, spans[half]],
            send_sem=gather_out.at[half, j],
            recv_sem=gather_in.at[half, j],
            device_id={"seq": side(j)},
            **place,
        )

    def up(half, j):
        sums, layered = ((sums_a, layers_a), (sums_b, layers_b))[half]
        return pltpu.make_async_remote_copy(
            src_ref=sums.at[lax.rem(layer + j, layers)],
            dst_ref=layered.at[layer],
            send_sem=up_out.at[half, j],
            recv_sem=up_in.at[half, j],
            device_id={"seq": over(j)},
            **place,
        )

    def give_back(half, j):
        scanned, before = ((scanned_a, before_a), (scanned_b, before_b))[half]
        return pltpu.make_async_remote_copy(
            src_ref=scanned.at[lax.rem(layer + j, layers)],
            dst_ref=before.at[layer],
            send_sem=back_out.at[half, j],
            recv_sem=back_in.at[half, j],
            device_id={"seq": over(j)},
            **place,
        )

    def spread(half, j):
        members = (members_a, members_b)[half]
        return pltpu.make_async_remote_copy(
            src_ref=members.at[lax.rem(member + j, ROW)],
            dst_ref=entry.at[member, half],
            send_sem=spread_out.at[half, j],
            recv_sem=spread_in.at[half, j],
            device_id={"seq": side(j)},
            **place,
        )

    order = (1, 3, 2)
    far = tuple(j for j in (1, 7, 2, 6, 3, 5, 4) if j < layers)
    for half in range(2):
        for j in order:
            gather(half, j).start()
    rows_in[member] = send[member]
    zero = jnp.zeros((HEAD // 8, 8, STATE), F32)

    def part(source, h, half):
        at = h * HEAD + half * (channels + 8 * heads)
        return rows_in[source, pl.ds(pl.multiple_of(at, 8), HEAD), :].reshape(HEAD // 8, 8, STATE)

    def decay(source, h):
        return rows_in[source, pl.ds(pl.multiple_of(channels + 8 * h, 8), 8), :]

    def turned(lap, count):
        return lap + down * (count - 1 - 2 * lap)

    for half in range(2):
        sums, layered, scanned, before, members = (
            (sums_a, layers_a, scanned_a, before_a, members_a),
            (sums_b, layers_b, scanned_b, before_b, members_b),
        )[half]
        for j in order:
            gather(half, j).wait_recv()

        def total(h, carry):
            state = zero
            through = jnp.ones((8, STATE), F32)
            for m in range(ROW):
                source = turned(m, ROW)
                step = decay(source, h)
                state = state * step[None] + part(source, h, half)
                through = through * step
            sums[h // each, h % each, :HEAD, :] = state.reshape(HEAD, STATE)
            if half == 0:
                sums[h // each, h % each, HEAD:, :] = through
            return carry

        lax.fori_loop(0, heads, total, 0)
        for j in far:
            up(half, j).start()
        layered[layer] = sums[layer]
        for j in far:
            up(half, j).wait_recv()
        for e in range(each):

            def scan(lap, state):
                at = turned(lap, layers)
                scanned[at, e] = state.reshape(HEAD, STATE)
                step = layers_a[at, e, HEAD:, :]
                return state * step[None] + layered[at, e, :HEAD, :].reshape(HEAD // 8, 8, STATE)

            lax.fori_loop(0, layers, scan, zero)
        for j in far:
            give_back(half, j).start()
        before[layer] = scanned[layer]
        for j in far:
            give_back(half, j).wait_recv()

        def unfold(h, carry):
            state = before[h // each, h % each].reshape(HEAD // 8, 8, STATE)
            for m in range(ROW):
                target = turned(m, ROW)
                members[target, pl.ds(pl.multiple_of(h * HEAD, 8), HEAD), :] = state.reshape(HEAD, STATE)
                if m < ROW - 1:
                    state = state * decay(target, h)[None] + part(target, h, half)
            return carry

        lax.fori_loop(0, heads, unfold, 0)
        for j in order:
            spread(half, j).start()
        entry[member, half] = members[member]
    for half in range(2):
        for j in order:
            spread(half, j).wait_recv()
    for half in range(2):
        for j in order:
            gather(half, j).wait_send()
            spread(half, j).wait_send()
        for j in far:
            up(half, j).wait_send()
            give_back(half, j).wait_send()


def finish_kernel(
    cot_hbm,
    ccot_hbm,
    entry,
    values,
    keys,
    dts,
    sigs,
    params,
    mixed,
    cmixed,
    d_val,
    d_key_high,
    d_key_low,
    d_raw_high,
    d_raw_low,
    cot,
    ccot,
    sems,
):
    fetches = [
        pltpu.make_async_copy(cot_hbm, cot, sems.at[0]),
        pltpu.make_async_copy(ccot_hbm, ccot, sems.at[1]),
    ]
    for fetch in fetches:
        fetch.start()
    channels = values.shape[1]
    heads = channels // HEAD
    rate, skip = params[1:2, :], params[2:3, :]
    spread = spread_matrix(channels)
    row_id, col_id = iota((ROWS, ROWS), 0), iota((ROWS, ROWS), 1)
    diagonal, lower, upper = row_id == col_id, row_id > col_id, row_id < col_id
    eye = where01(diagonal)
    twice = jnp.where(diagonal, 2.0, 1.0)
    lane_first = where01(iota((1, 2 * HEAD), 1) < HEAD, BF16)
    lane_second = where01(iota((1, 2 * HEAD), 1) >= HEAD, BF16)
    head_lane = iota((ROWS, LANES), 1)
    head_row = iota((heads, ROWS), 0)
    widen = lambda w: dot(w, spread, precision=HIGHEST)
    narrow = lambda w: dot(w, spread, 1, 1, precision=HIGHEST)
    skip_wide = widen(skip)
    for s in range(2):
        rows = slice(s * ROWS, (s + 1) * ROWS)
        dt = dts[rows, :]
        log_decay, before, upto, total = decay_parts(dt, rate)
        dt_t = dot(dt, eye, 0, 0, precision=HIGHEST)
        before_t = dot(log_decay, where01(upper), 0, 0, precision=HIGHEST)
        upto_t = before_t + dot(log_decay, eye, 0, 0, precision=HIGHEST)
        fetches[s].wait()
        x_b, g_b = values[rows, :], (cot if s == 0 else ccot)[...]
        x, g = x_b.astype(F32), g_b.astype(F32)
        write, read = keys[rows, :STATE], keys[rows, STATE:]
        u_fwd, u_bwd = widen(jnp.exp(total - upto)), widen(jnp.exp(before))
        w_fwd, w_bwd = widen(jnp.exp(upto)), widen(jnp.exp(total - before))
        dt_wide = widen(dt)
        h_in, m_in, k_in, l_in = entry[s, 0], entry[s, 1], entry[2 + s, 0], entry[2 + s, 1]
        y_fwd = w_fwd * dot_right(read, h_in, 1, 1)
        y_bwd = w_bwd * dot_right(read, k_in, 1, 1)
        x_l = u_fwd * dot_right(write, l_in, 1, 1)
        x_m = u_bwd * dot_right(write, m_in, 1, 1)
        d_read = dot_both(w_fwd * g, h_in) + dot_both(w_bwd * g, k_in)
        d_write = dot_both(u_fwd * dt_wide * x, l_in) + dot_both(u_bwd * dt_wide * x, m_in)
        r_fwd, r_bwd = narrow(g * y_fwd), narrow(g * y_bwd)
        q_fwd, q_bwd = narrow(x * x_l), narrow(x * x_m)
        both = dot(spread, l_in * h_in + m_in * k_in, precision=HIGHEST)
        both = dot(jnp.ones((8, STATE), F32), both, 1, 1, precision=HIGHEST)[0:1]
        scores = dot(read, write, 1, 1)
        d_scores = jnp.zeros((ROWS, ROWS), F32)
        by_row = jnp.zeros((ROWS, LANES), F32)
        by_row_up = jnp.zeros((ROWS, LANES), F32)
        direct_t = jnp.zeros((heads, ROWS), F32)
        low_t = jnp.zeros((heads, ROWS), F32)
        up_t = jnp.zeros((heads, ROWS), F32)
        for pair in range(heads // 2):
            lanes = slice(pair * 2 * HEAD, (pair + 1) * 2 * HEAD)
            x_pair, g_pair = x_b[:, lanes], g_b[:, lanes]
            y_pair = jnp.zeros((ROWS, 2 * HEAD), F32)
            d_pair = jnp.zeros((ROWS, 2 * HEAD), F32)
            for half, lane_mask in ((0, lane_first), (1, lane_second)):
                h = pair * 2 + half
                x_h, g_h = x_pair * lane_mask, g_pair * lane_mask
                gap = jnp.where(
                    upper,
                    before_t[h : h + 1, :] - before[:, h : h + 1],
                    upto[:, h : h + 1] - upto_t[h : h + 1, :],
                )
                decay = jnp.exp(jnp.minimum(gap, 0.0)) * twice
                dt_row = dt_t[h : h + 1, :]
                scaled = scores * decay
                weights = scaled * dt_row
                w_high, w_low = split(weights)
                y_pair = y_pair + (dot(w_high, x_h) + dot(w_low, x_h))
                d_pair = d_pair + (dot(w_high, g_h, 0, 0) + dot(w_low, g_h, 0, 0))
                outer = dot(g_h, x_pair, 1, 1)
                grads = outer * scaled
                d_scores = d_scores + outer * (decay * dt_row)
                q = grads * dt_row
                q_low, q_up = jnp.where(lower, q, 0.0), jnp.where(upper, q, 0.0)
                by_row = jnp.where(head_lane == h, jnp.sum(q_low, 1, keepdims=True), by_row)
                by_row_up = jnp.where(head_lane == h, jnp.sum(q_up, 1, keepdims=True), by_row_up)
                direct_t = jnp.where(head_row == h, jnp.sum(grads, 0, keepdims=True), direct_t)
                low_t = jnp.where(head_row == h, jnp.sum(q_low, 0, keepdims=True), low_t)
                up_t = jnp.where(head_row == h, jnp.sum(q_up, 0, keepdims=True), up_t)
            out = y_pair + y_fwd[:, lanes] + y_bwd[:, lanes] + skip_wide[:, lanes] * x[:, lanes]
            (mixed if s == 0 else cmixed)[:, lanes] = out.astype(BF16)
            grad = d_pair + dt_wide[:, lanes] * (x_l[:, lanes] + x_m[:, lanes])
            grad = grad + skip_wide[:, lanes] * g[:, lanes]
            d_val[rows, lanes] = grad.astype(BF16)
        stacked = (direct_t, low_t, up_t, jnp.zeros((ROWS - 3 * heads, ROWS), F32))
        turned = jnp.transpose(jnp.concatenate(stacked, 0))
        picked = lambda at: jnp.where(head_lane < heads, pltpu.roll(turned, LANES - at, 1) if at else turned, 0.0)
        d_dt = picked(0) + q_fwd + q_bwd
        d_upto = by_row - picked(heads) + r_fwd - dt * q_fwd
        d_before = picked(2 * heads) - by_row_up - r_bwd + dt * q_bwd
        d_total = jnp.sum(r_bwd + dt * q_fwd, 0, keepdims=True) + jnp.exp(total) * both
        from_here = where01(row_id <= col_id)
        d_log = dot(from_here, d_upto, precision=HIGHEST) + dot(where01(upper), d_before, precision=HIGHEST)
        d_log = d_log + d_total
        d_raw_high[rows, :], d_raw_low[rows, :] = split((d_dt - rate * d_log) * sigs[rows, :])
        d_write = d_write + dot_left(d_scores, read, 0, 0)
        d_read = d_read + dot_left(d_scores, write)
        d_key_high[rows, :STATE], d_key_low[rows, :STATE] = split(d_write)
        d_key_high[rows, STATE:], d_key_low[rows, STATE:] = split(d_read)


def reduce_kernel(
    ranks,
    inner_hbm,
    select_hbm,
    step_hbm,
    d_val,
    d_key_high,
    d_key_low,
    d_raw_high,
    d_raw_low,
    first,
    second,
    inner,
    select,
    step,
    step_wide,
    term,
    arrived,
    sems,
    send_sems,
    recv_sems,
):
    fetches = [
        pltpu.make_async_copy(inner_hbm, inner, sems.at[0]),
        pltpu.make_async_copy(select_hbm, select, sems.at[1]),
        pltpu.make_async_copy(step_hbm, step, sems.at[2]),
    ]
    for fetch in fetches:
        fetch.start()
    me = lax.axis_index("chan")
    width = term.shape[2]
    heads = step.shape[0]
    barrier = pltpu.get_barrier_semaphore()
    for j in range(1, ranks):
        pl.semaphore_signal(
            barrier, inc=1, device_id={"chan": lax.rem(me + j, ranks)}, device_id_type=pl.DeviceIdType.MESH
        )
    step_wide[...] = jnp.zeros_like(step_wide)
    for fetch in fetches:
        fetch.wait()
    step_wide[:heads, :] = step[...]

    def chunk(rows, rank):
        at = pl.multiple_of(rank * width, width)
        cols = pl.ds(at, width)
        part = dot(d_val[rows, :], inner[cols, :], 1, 1)
        keys = select[cols, :]
        part = part + (dot(d_key_high[rows, :], keys, 1, 1) + dot(d_key_low[rows, :], keys, 1, 1))
        steps = step_wide[:, cols]
        return part + (dot(d_raw_high[rows, :], steps) + dot(d_raw_low[rows, :], steps))

    def share(rank):
        term[rank, :ROWS, :] = chunk(slice(0, ROWS), rank)
        term[rank, ROWS:, :] = chunk(slice(ROWS, 2 * ROWS), ranks - 1 - rank)

    def copy(j):
        peer = lax.rem(me + j, ranks)
        return pltpu.make_async_remote_copy(
            src_ref=term.at[peer],
            dst_ref=arrived.at[me],
            send_sem=send_sems.at[j],
            recv_sem=recv_sems.at[j],
            device_id={"chan": peer},
            device_id_type=pl.DeviceIdType.MESH,
        )

    share(lax.rem(me + 1, ranks))
    pl.semaphore_wait(barrier, ranks - 1)
    copy(1).start()
    for j in range(2, ranks):
        share(lax.rem(me + j, ranks))
        copy(j).start()
    share(me)
    total = term[me]
    for j in range(1, ranks):
        copy(j).wait_recv()
        total = total + arrived[lax.rem(me + ranks - j, ranks)]
    for j in range(1, ranks):
        copy(j).wait_send()
    total = total.astype(BF16)
    first[...] = total[:ROWS]
    anti = anti_identity()
    blocks = width // FLIP
    for b in range(blocks):
        block = total[ROWS:, (blocks - 1 - b) * FLIP : (blocks - b) * FLIP]
        second[:, b * FLIP : (b + 1) * FLIP] = dot(block, anti).astype(BF16)


def call(kernel, outs, args, scratch=(), far=0, **params):
    whole = pl.BlockSpec(memory_space=pltpu.VMEM)
    return pl.pallas_call(
        kernel,
        out_shape=[jax.ShapeDtypeStruct(shape, dtype) for shape, dtype in outs],
        in_specs=[pl.BlockSpec(memory_space=pltpu.HBM)] * far + [whole] * (len(args) - far),
        out_specs=[whole] * len(outs),
        scratch_shapes=list(scratch),
        compiler_params=pltpu.CompilerParams(vmem_limit_bytes=48 << 20, **params),
    )(*[pltpu.with_memory_space_constraint(a, pltpu.HBM) for a in args[:far]], *args[far:])


def local(hidden, complement, inner, select, step, bias, rate, skip, cot, ccot):
    shards, ranks = lax.axis_size("seq"), lax.axis_size("chan")
    heads = bias.shape[0]
    depth = hidden.shape[1]
    channels = heads * HEAD
    params = jnp.pad(jnp.stack([bias, rate, skip]), ((0, 5), (0, LANES - heads)))
    step = step.T
    send, values, keys, dts, sigs = call(
        project_kernel,
        [
            ((4, 2 * channels + 8 * heads, STATE), F32),
            ((2 * ROWS, channels), BF16),
            ((2 * ROWS, 2 * STATE), BF16),
            ((2 * ROWS, LANES), F32),
            ((2 * ROWS, LANES), F32),
        ],
        (hidden, complement, inner, select, cot, ccot, step, params),
        [
            pltpu.VMEM((2 * ROWS, depth), BF16),
            pltpu.VMEM((LANES, depth), BF16),
            pltpu.VMEM((ROWS, depth), BF16),
            pltpu.VMEM(inner.shape, BF16),
            pltpu.VMEM(select.shape, BF16),
            pltpu.VMEM(cot.shape, BF16),
            pltpu.VMEM(ccot.shape, BF16),
            pltpu.VMEM(step.shape, BF16),
            pltpu.SemaphoreType.DMA((7,)),
        ],
        far=7,
    )
    layers = shards // ROW
    each = heads // layers
    halves = lambda rows: pltpu.VMEM((layers, each, rows, STATE), F32)
    dma = lambda count: pltpu.SemaphoreType.DMA((2, count))
    (entry,) = call(
        functools.partial(exchange_kernel, layers, heads),
        [((4, 2, channels, STATE), F32)],
        (send,),
        [
            pltpu.VMEM(send.shape, F32),
            halves(HEAD + 8),
            halves(HEAD),
            halves(HEAD + 8),
            halves(HEAD),
            halves(HEAD),
            halves(HEAD),
            halves(HEAD),
            halves(HEAD),
            pltpu.VMEM((ROW, channels, STATE), F32),
            pltpu.VMEM((ROW, channels, STATE), F32),
            dma(ROW),
            dma(ROW),
            dma(layers),
            dma(layers),
            dma(layers),
            dma(layers),
            dma(ROW),
            dma(ROW),
        ],
        collective_id=2,
        has_side_effects=True,
    )
    mixed, cmixed, *grads = call(
        finish_kernel,
        [
            ((ROWS, channels), BF16),
            ((ROWS, channels), BF16),
            ((2 * ROWS, channels), BF16),
            ((2 * ROWS, 2 * STATE), BF16),
            ((2 * ROWS, 2 * STATE), BF16),
            ((2 * ROWS, LANES), BF16),
            ((2 * ROWS, LANES), BF16),
        ],
        (cot, ccot, entry, values, keys, dts, sigs, params),
        [pltpu.VMEM(cot.shape, BF16), pltpu.VMEM(ccot.shape, BF16), pltpu.SemaphoreType.DMA((2,))],
        far=2,
    )
    share = (ranks, 2 * ROWS, depth // ranks)
    first, second = call(
        functools.partial(reduce_kernel, ranks),
        [((ROWS, depth // ranks), BF16)] * 2,
        (inner, select, step, *grads),
        [
            pltpu.VMEM(inner.shape, BF16),
            pltpu.VMEM(select.shape, BF16),
            pltpu.VMEM(step.shape, BF16),
            pltpu.VMEM((LANES, depth), BF16),
            pltpu.VMEM(share, F32),
            pltpu.VMEM(share, F32),
            pltpu.SemaphoreType.DMA((3,)),
            pltpu.SemaphoreType.DMA((ranks,)),
            pltpu.SemaphoreType.DMA((ranks,)),
        ],
        far=3,
        collective_id=1,
        has_side_effects=True,
    )
    return mixed, cmixed, first, second


def solution(mesh):
    rows = P(("dp", "seq"), None)
    tiles = P(("dp", "seq"), "chan")
    in_specs = (rows, rows, P(None, "chan"), P(), P(None, "chan"), P("chan"), P("chan"), P("chan"), tiles, tiles)
    return jax.shard_map(
        local, mesh=mesh, in_specs=in_specs, out_specs=(tiles,) * 4, check_vma=False
    )
```

```python
import functools

import jax
import jax.numpy as jnp
from jax import lax
from jax.experimental import pallas as pl
from jax.experimental.pallas import tpu as pltpu
from jax.sharding import PartitionSpec as P

F32 = jnp.float32
BF16 = jnp.bfloat16
HIGHEST = lax.Precision.HIGHEST
HEAD = 64
STATE = 128
ROWS = 128
FLIP = 256
LANES = 128
ROW = 4


def dot(a, b, ca=1, cb=0, precision=None):
    return lax.dot_general(
        a, b, (((ca,), (cb,)), ((), ())), precision=precision, preferred_element_type=F32
    )


def split(a):
    high = a.astype(BF16)
    return high, (a - high.astype(F32)).astype(BF16)


def dot_left(a, b, ca=1, cb=0):
    high, low = split(a)
    return dot(high, b, ca, cb) + dot(low, b, ca, cb)


def dot_right(a, b, ca=1, cb=0):
    high, low = split(b)
    return dot(a, high, ca, cb) + dot(a, low, ca, cb)


def dot_both(a, b, ca=1, cb=0):
    a_high, a_low = split(a)
    b_high, b_low = split(b)
    return dot(a_high, b_high, ca, cb) + (dot(a_high, b_low, ca, cb) + dot(a_low, b_high, ca, cb))


def iota(shape, dim):
    return lax.broadcasted_iota(jnp.int32, shape, dim)


def where01(mask, dtype=F32):
    return jnp.where(mask, 1.0, 0.0).astype(dtype)


def anti_identity():
    return where01(iota((FLIP, FLIP), 0) + iota((FLIP, FLIP), 1) == FLIP - 1, BF16)


def spread_matrix(channels):
    lanes = iota((LANES, channels), 1)
    row = iota((LANES, channels), 0) * HEAD
    return where01((lanes >= row) & (lanes < row + HEAD), BF16)


def decay_parts(dt, rate):
    log_decay = -dt * rate
    strict = where01(iota((ROWS, ROWS), 0) > iota((ROWS, ROWS), 1))
    before = dot(strict, log_decay, precision=HIGHEST)
    upto = before + log_decay
    total = upto[ROWS - 1 : ROWS, :]
    return log_decay, before, upto, total


def project_kernel(
    hidden_hbm,
    complement_hbm,
    inner_hbm,
    select_hbm,
    cot_hbm,
    ccot_hbm,
    step_hbm,
    params,
    send,
    values,
    keys,
    dts,
    sigs,
    source,
    step_wide,
    complement,
    inner,
    select,
    cot,
    ccot,
    step,
    sems,
):
    channels = inner.shape[1]
    heads = channels // HEAD
    bias, rate = params[0:1, :], params[1:2, :]
    fetches = [
        pltpu.make_async_copy(here, there, sems.at[i])
        for i, (here, there) in enumerate(
            (
                (complement_hbm, complement),
                (hidden_hbm, source.at[:ROWS]),
                (select_hbm, select),
                (inner_hbm, inner),
                (cot_hbm, cot),
                (ccot_hbm, ccot),
                (step_hbm, step),
            )
        )
    ]
    for fetch in fetches:
        fetch.start()
    depth = complement.shape[1]
    blocks = depth // FLIP
    anti = anti_identity()
    fetches[0].wait()
    for b in range(blocks):
        block = complement[:, (blocks - 1 - b) * FLIP : (blocks - b) * FLIP]
        source[ROWS:, b * FLIP : (b + 1) * FLIP] = dot(block, anti).astype(BF16)
    step_wide[...] = jnp.zeros_like(step_wide)
    fetches[6].wait()
    step_wide[:heads, :] = step[...]
    fetches[1].wait()
    src = source[...]
    raw = dot(src, step_wide[...], 1, 1) + bias
    fetches[2].wait()
    k_all = dot(src, select[...]).astype(BF16)
    fetches[3].wait()
    v_all = dot(src, inner[...]).astype(BF16)
    fetches[4].wait()
    fetches[5].wait()
    small = jnp.exp(-jnp.abs(raw))
    one_more = 1.0 + small
    tail = jnp.where(
        one_more == 1.0, small, jnp.log(one_more) * (small / jnp.where(one_more == 1.0, 1.0, one_more - 1.0))
    )
    dt_all = jnp.maximum(raw, 0.0) + tail
    values[...] = v_all
    keys[...] = k_all
    dts[...] = dt_all
    sigs[...] = jnp.where(raw >= 0.0, 1.0, small) / one_more
    spread = spread_matrix(channels)
    ones = jnp.ones((ROWS, STATE), F32)
    for s in range(2):
        rows = slice(s * ROWS, (s + 1) * ROWS)
        dt = dt_all[rows]
        log_decay, before, upto, total = decay_parts(dt, rate)
        x = v_all[rows].astype(F32)
        g = (cot if s == 0 else ccot)[...].astype(F32)
        write, read = k_all[rows, :STATE], k_all[rows, STATE:]
        widen = lambda w: dot_left(w, spread)
        pieces = (
            (0, 0, widen(jnp.exp(total - upto) * dt) * x, write),
            (0, 1, widen(jnp.exp(total - before)) * g, read),
            (1, 0, widen(jnp.exp(before) * dt) * x, write),
            (1, 1, widen(jnp.exp(upto)) * g, read),
        )
        for way, kind, left, right in pieces:
            state = dot_left(left, right, 0, 0)
            send[way * 2 + kind, s, :channels, :] = state
        decay = jnp.exp(dot(log_decay, ones, 0, 0, precision=HIGHEST))
        for q in range(ROW):
            for h in range(heads):
                at = channels + 8 * h
                send[q, s, at : at + 8, :] = jnp.broadcast_to(decay[h : h + 1], (8, STATE))


def within_chunk(s, values, keys, dts, rate, g_b, y_in, d_in, key_in, row_sums, column_sums):
    heads = values.shape[1] // HEAD
    row_id, col_id = iota((ROWS, ROWS), 0), iota((ROWS, ROWS), 1)
    diagonal, lower, upper = row_id == col_id, row_id > col_id, row_id < col_id
    eye = where01(diagonal)
    twice = jnp.where(diagonal, 2.0, 1.0)
    lane_first = where01(iota((1, 2 * HEAD), 1) < HEAD, BF16)
    lane_second = where01(iota((1, 2 * HEAD), 1) >= HEAD, BF16)
    head_lane = iota((ROWS, LANES), 1)
    rows = slice(s * ROWS, (s + 1) * ROWS)
    dt = dts[rows, :]
    log_decay, before, upto, total = decay_parts(dt, rate)
    dt_t = dot(dt, eye, 0, 0, precision=HIGHEST)
    before_t = dot(log_decay, where01(upper), 0, 0, precision=HIGHEST)
    upto_t = before_t + dot(log_decay, eye, 0, 0, precision=HIGHEST)
    write, read = keys[rows, :STATE], keys[rows, STATE:]
    scores = dot(read, write, 1, 1)
    d_scores = jnp.zeros((ROWS, ROWS), F32)
    by_row = jnp.zeros((ROWS, LANES), F32)
    by_row_up = jnp.zeros((ROWS, LANES), F32)
    for pair in range(heads // 2):
        lanes = slice(pair * 2 * HEAD, (pair + 1) * 2 * HEAD)
        x_pair, g_pair = values[rows, lanes], g_b[:, lanes]
        y_pair = jnp.zeros((ROWS, 2 * HEAD), F32)
        d_pair = jnp.zeros((ROWS, 2 * HEAD), F32)
        for half, lane_mask in ((0, lane_first), (1, lane_second)):
            h = pair * 2 + half
            x_h, g_h = x_pair * lane_mask, g_pair * lane_mask
            gap = jnp.where(
                upper,
                before_t[h : h + 1, :] - before[:, h : h + 1],
                upto[:, h : h + 1] - upto_t[h : h + 1, :],
            )
            decay = jnp.exp(jnp.minimum(gap, 0.0)) * twice
            dt_row = dt_t[h : h + 1, :]
            scaled = scores * decay
            w_high, w_low = split(scaled * dt_row)
            y_pair = y_pair + (dot(w_high, x_h) + dot(w_low, x_h))
            d_pair = d_pair + (dot(w_high, g_h, 0, 0) + dot(w_low, g_h, 0, 0))
            outer = dot(g_h, x_pair, 1, 1)
            grads = outer * scaled
            d_scores = d_scores + outer * (decay * dt_row)
            q = grads * dt_row
            q_low, q_up = jnp.where(lower, q, 0.0), jnp.where(upper, q, 0.0)
            by_row = jnp.where(head_lane == h, jnp.sum(q_low, 1, keepdims=True), by_row)
            by_row_up = jnp.where(head_lane == h, jnp.sum(q_up, 1, keepdims=True), by_row_up)
            column_sums[s, h : h + 1, :] = jnp.sum(grads, 0, keepdims=True)
            column_sums[s, heads + h : heads + h + 1, :] = jnp.sum(q_low, 0, keepdims=True)
            column_sums[s, 2 * heads + h : 2 * heads + h + 1, :] = jnp.sum(q_up, 0, keepdims=True)
        y_in[rows, lanes] = y_pair
        d_in[rows, lanes] = d_pair
    row_sums[s, 0] = by_row
    row_sums[s, 1] = by_row_up
    key_in[rows, :STATE] = dot_left(d_scores, read, 0, 0)
    key_in[rows, STATE:] = dot_left(d_scores, write)


def finish(
    s,
    entry,
    values,
    keys,
    dts,
    sigs,
    params,
    g_b,
    y_in,
    d_in,
    key_in,
    row_sums,
    column_sums,
    mixed,
    d_val,
    d_key_high,
    d_key_low,
    d_raw_high,
    d_raw_low,
):
    channels = values.shape[1]
    heads = channels // HEAD
    rate, skip = params[1:2, :], params[2:3, :]
    spread = spread_matrix(channels)
    row_id, col_id = iota((ROWS, ROWS), 0), iota((ROWS, ROWS), 1)
    widen = lambda w: dot_left(w, spread)
    narrow = lambda w: dot_left(w, spread, 1, 1)
    skip_wide = widen(skip)
    rows = slice(s * ROWS, (s + 1) * ROWS)
    dt = dts[rows, :]
    log_decay, before, upto, total = decay_parts(dt, rate)
    x, g = values[rows, :].astype(F32), g_b.astype(F32)
    write, read = keys[rows, :STATE], keys[rows, STATE:]
    u_fwd, u_bwd = widen(jnp.exp(total - upto)), widen(jnp.exp(before))
    w_fwd, w_bwd = widen(jnp.exp(upto)), widen(jnp.exp(total - before))
    dt_wide = widen(dt)
    h_in, m_in, k_in, l_in = entry[0, s], entry[1, s], entry[2, s], entry[3, s]
    y_fwd = w_fwd * dot_right(read, h_in, 1, 1)
    y_bwd = w_bwd * dot_right(read, k_in, 1, 1)
    x_l = u_fwd * dot_right(write, l_in, 1, 1)
    x_m = u_bwd * dot_right(write, m_in, 1, 1)
    d_read = dot_both(w_fwd * g, h_in) + dot_both(w_bwd * g, k_in)
    d_write = dot_both(u_fwd * dt_wide * x, l_in) + dot_both(u_bwd * dt_wide * x, m_in)
    r_fwd, r_bwd = narrow(g * y_fwd), narrow(g * y_bwd)
    q_fwd, q_bwd = narrow(x * x_l), narrow(x * x_m)
    both = dot_right(spread, l_in * h_in + m_in * k_in)
    both = dot(jnp.ones((8, STATE), F32), both, 1, 1, precision=HIGHEST)[0:1]
    out = y_in[rows, :] + y_fwd + y_bwd + skip_wide * x
    mixed[...] = out.astype(BF16)
    d_val[rows, :] = (d_in[rows, :] + dt_wide * (x_l + x_m) + skip_wide * g).astype(BF16)
    sums = column_sums[s]
    picked = lambda at: dot_left(sums, where01((row_id == col_id + at) & (col_id < heads), BF16), 0, 0)
    d_dt = picked(0) + q_fwd + q_bwd
    d_upto = row_sums[s, 0] - picked(heads) + r_fwd - dt * q_fwd
    d_before = picked(2 * heads) - row_sums[s, 1] - r_bwd + dt * q_bwd
    d_total = jnp.sum(r_bwd + dt * q_fwd, 0, keepdims=True) + jnp.exp(total) * both
    d_log = dot(where01(row_id <= col_id), d_upto, precision=HIGHEST)
    d_log = d_log + dot(where01(row_id < col_id), d_before, precision=HIGHEST) + d_total
    d_raw_high[rows, :], d_raw_low[rows, :] = split((d_dt - rate * d_log) * sigs[rows, :])
    d_key_high[rows, :STATE], d_key_low[rows, :STATE] = split(d_write + key_in[rows, :STATE])
    d_key_high[rows, STATE:], d_key_low[rows, STATE:] = split(d_read + key_in[rows, STATE:])


def main_kernel(
    layers,
    ranks,
    cot_hbm,
    ccot_hbm,
    inner_hbm,
    select_hbm,
    step_hbm,
    send,
    values,
    keys,
    dts,
    sigs,
    params,
    mixed,
    cmixed,
    first,
    second,
    cot,
    ccot,
    inner,
    select,
    step,
    step_wide,
    entry,
    y_in,
    d_in,
    key_in,
    row_sums,
    column_sums,
    d_val,
    d_key_high,
    d_key_low,
    d_raw_high,
    d_raw_low,
    rows_in,
    sums,
    layered,
    scanned,
    before,
    members,
    term,
    shares,
    sems,
    gather_out,
    gather_in,
    up_out,
    up_in,
    back_out,
    back_in,
    spread_out,
    spread_in,
    share_out,
    share_in,
):
    fetches = [
        pltpu.make_async_copy(here, there, sems.at[i])
        for i, (here, there) in enumerate(
            ((cot_hbm, cot), (ccot_hbm, ccot), (inner_hbm, inner), (select_hbm, select), (step_hbm, step))
        )
    ]
    for fetch in fetches:
        fetch.start()
    me, rank = lax.axis_index("seq"), lax.axis_index("chan")
    channels = values.shape[1]
    heads = channels // HEAD
    width = term.shape[3]
    layer, member = me // ROW, lax.rem(me, ROW)
    down = member // 2
    each = heads // layers
    side = lambda j: layer * ROW + lax.rem(member + j, ROW)
    over = lambda j: lax.rem(layer + j, layers) * ROW + member
    across = lambda j: lax.rem(rank + j, ranks)
    place = {"device_id_type": pl.DeviceIdType.MESH}
    barrier = pltpu.get_barrier_semaphore()
    for j in range(1, ROW):
        pl.semaphore_signal(barrier, inc=1, device_id={"seq": side(j)}, **place)
    for j in range(1, layers):
        pl.semaphore_signal(barrier, inc=1, device_id={"seq": over(j)}, **place)
    for j in range(1, ranks):
        pl.semaphore_signal(barrier, inc=1, device_id={"chan": across(j)}, **place)
    pl.semaphore_wait(barrier, ROW + layers + ranks - 3)

    def copy(here, there, sent, got, device):
        return pltpu.make_async_remote_copy(
            src_ref=here, dst_ref=there, send_sem=sent, recv_sem=got, device_id=device, **place
        )

    def gather(half, j):
        peer = lax.rem(member + j, ROW)
        there = rows_in.at[member, half]
        return copy(send.at[peer, half], there, gather_out.at[half, j], gather_in.at[half, j], {"seq": side(j)})

    def up(half, j):
        peer = lax.rem(layer + j, layers)
        there = layered.at[half, layer]
        return copy(sums.at[half, peer], there, up_out.at[half, j], up_in.at[half, j], {"seq": over(j)})

    def give_back(half, j):
        peer = lax.rem(layer + j, layers)
        there = before.at[half, layer]
        return copy(scanned.at[half, peer], there, back_out.at[half, j], back_in.at[half, j], {"seq": over(j)})

    def spread(half, j):
        peer = lax.rem(member + j, ROW)
        there = entry.at[member, half]
        return copy(members.at[half, peer], there, spread_out.at[half, j], spread_in.at[half, j], {"seq": side(j)})

    def share(half, j):
        there = shares.at[half, rank]
        return copy(term.at[half, across(j)], there, share_out.at[half, j], share_in.at[half, j], {"chan": across(j)})

    order = (1, 3, 2)
    far = tuple(j for j in (1, 7, 2, 6, 3, 5, 4) if j < layers)
    for half in range(2):
        for j in order:
            gather(half, j).start()
    rows_in[member] = send[member]
    column_sums[...] = jnp.zeros_like(column_sums)
    step_wide[...] = jnp.zeros_like(step_wide)
    for s, g in ((0, cot), (1, ccot)):
        fetches[s].wait()
        within_chunk(s, values, keys, dts, params[1:2, :], g[...], y_in, d_in, key_in, row_sums, column_sums)
    for fetch in fetches[2:]:
        fetch.wait()
    step_wide[:heads, :] = step[...]
    zero = jnp.zeros((HEAD // 8, 8, STATE), F32)

    def part(source, h, half):
        return rows_in[source, half, pl.ds(pl.multiple_of(h * HEAD, 8), HEAD), :].reshape(HEAD // 8, 8, STATE)

    def decay(source, h, half):
        return rows_in[source, half, pl.ds(pl.multiple_of(channels + 8 * h, 8), 8), :]

    def turned(lap, count):
        return lap + down * (count - 1 - 2 * lap)

    for half in range(2):
        for j in order:
            gather(half, j).wait_recv()

        def total(h, carry):
            state = zero
            through = jnp.ones((8, STATE), F32)
            for m in range(ROW):
                source = turned(m, ROW)
                slower = decay(source, h, half)
                state = state * slower[None] + part(source, h, half)
                through = through * slower
            sums[half, h // each, h % each, :HEAD, :] = state.reshape(HEAD, STATE)
            sums[half, h // each, h % each, HEAD:, :] = through
            return carry

        lax.fori_loop(0, heads, total, 0)
        for j in far:
            up(half, j).start()
        layered[half, layer] = sums[half, layer]
        for j in far:
            up(half, j).wait_recv()
        for e in range(each):

            def scan(lap, state):
                at = turned(lap, layers)
                scanned[half, at, e] = state.reshape(HEAD, STATE)
                slower = layered[half, at, e, HEAD:, :]
                return state * slower[None] + layered[half, at, e, :HEAD, :].reshape(HEAD // 8, 8, STATE)

            lax.fori_loop(0, layers, scan, zero)
        for j in far:
            give_back(half, j).start()
        before[half, layer] = scanned[half, layer]
        for j in far:
            give_back(half, j).wait_recv()

        def unfold(h, carry):
            state = before[half, h // each, h % each].reshape(HEAD // 8, 8, STATE)
            for m in range(ROW):
                target = turned(m, ROW)
                members[half, target, pl.ds(pl.multiple_of(h * HEAD, 8), HEAD), :] = state.reshape(HEAD, STATE)
                if m < ROW - 1:
                    state = state * decay(target, h, half)[None] + part(target, h, half)
            return carry

        lax.fori_loop(0, heads, unfold, 0)
        for j in order:
            spread(half, j).start()
        entry[member, half] = members[half, member]

    def chunk(half, block):
        rows = slice(half * ROWS, (half + 1) * ROWS)
        cols = pl.ds(pl.multiple_of(block * width, width), width)
        value = dot(d_val[rows, :], inner[cols, :], 1, 1)
        picked = select[cols, :]
        value = value + (dot(d_key_high[rows, :], picked, 1, 1) + dot(d_key_low[rows, :], picked, 1, 1))
        steps = step_wide[:, cols]
        return value + (dot(d_raw_high[rows, :], steps) + dot(d_raw_low[rows, :], steps))

    for s, g, out in ((0, cot, mixed), (1, ccot, cmixed)):
        for j in order:
            spread(s, j).wait_recv()
        finish(
            s,
            entry,
            values,
            keys,
            dts,
            sigs,
            params,
            g[...],
            y_in,
            d_in,
            key_in,
            row_sums,
            column_sums,
            out,
            d_val,
            d_key_high,
            d_key_low,
            d_raw_high,
            d_raw_low,
        )
        for j in range(1, ranks + 1):
            peer = across(j)
            term[s, peer] = chunk(s, ranks - 1 - peer if s else peer)
            if j < ranks:
                share(s, j).start()
    anti = anti_identity()
    for s in range(2):
        result = term[s, rank]
        for j in range(1, ranks):
            share(s, j).wait_recv()
            result = result + shares[s, across(ranks - j)]
        result = result.astype(BF16)
        if s == 0:
            first[...] = result
        else:
            blocks = width // FLIP
            for b in range(blocks):
                block = result[:, (blocks - 1 - b) * FLIP : (blocks - b) * FLIP]
                second[:, b * FLIP : (b + 1) * FLIP] = dot(block, anti).astype(BF16)
    for half in range(2):
        for j in order:
            gather(half, j).wait_send()
            spread(half, j).wait_send()
        for j in far:
            up(half, j).wait_send()
            give_back(half, j).wait_send()
        for j in range(1, ranks):
            share(half, j).wait_send()


def call(kernel, outs, args, scratch=(), far=0, **params):
    whole = pl.BlockSpec(memory_space=pltpu.VMEM)
    return pl.pallas_call(
        kernel,
        out_shape=[jax.ShapeDtypeStruct(shape, dtype) for shape, dtype in outs],
        in_specs=[pl.BlockSpec(memory_space=pltpu.HBM)] * far + [whole] * (len(args) - far),
        out_specs=[whole] * len(outs),
        scratch_shapes=list(scratch),
        compiler_params=pltpu.CompilerParams(vmem_limit_bytes=48 << 20, **params),
    )(*[pltpu.with_memory_space_constraint(a, pltpu.HBM) for a in args[:far]], *args[far:])


def local(hidden, complement, inner, select, step, bias, rate, skip, cot, ccot):
    shards, ranks = lax.axis_size("seq"), lax.axis_size("chan")
    heads = bias.shape[0]
    depth = hidden.shape[1]
    channels = heads * HEAD
    params = jnp.pad(jnp.stack([bias, rate, skip]), ((0, 5), (0, LANES - heads)))
    step = step.T
    send, values, keys, dts, sigs = call(
        project_kernel,
        [
            ((ROW, 2, channels + 8 * heads, STATE), F32),
            ((2 * ROWS, channels), BF16),
            ((2 * ROWS, 2 * STATE), BF16),
            ((2 * ROWS, LANES), F32),
            ((2 * ROWS, LANES), F32),
        ],
        (hidden, complement, inner, select, cot, ccot, step, params),
        [
            pltpu.VMEM((2 * ROWS, depth), BF16),
            pltpu.VMEM((LANES, depth), BF16),
            pltpu.VMEM((ROWS, depth), BF16),
            pltpu.VMEM(inner.shape, BF16),
            pltpu.VMEM(select.shape, BF16),
            pltpu.VMEM(cot.shape, BF16),
            pltpu.VMEM(ccot.shape, BF16),
            pltpu.VMEM(step.shape, BF16),
            pltpu.SemaphoreType.DMA((7,)),
        ],
        far=7,
    )
    layers = shards // ROW
    each = heads // layers
    width = depth // ranks
    dma = lambda *count: pltpu.SemaphoreType.DMA(count)
    wide = lambda *shape: pltpu.VMEM(shape, F32)
    narrow = lambda *shape: pltpu.VMEM(shape, BF16)
    return call(
        functools.partial(main_kernel, layers, ranks),
        [((ROWS, channels), BF16)] * 2 + [((ROWS, width), BF16)] * 2,
        (cot, ccot, inner, select, step, send, values, keys, dts, sigs, params),
        [
            narrow(*cot.shape),
            narrow(*ccot.shape),
            narrow(*inner.shape),
            narrow(*select.shape),
            narrow(*step.shape),
            narrow(LANES, depth),
            wide(ROW, 2, channels, STATE),
            wide(2 * ROWS, channels),
            wide(2 * ROWS, channels),
            wide(2 * ROWS, 2 * STATE),
            wide(2, 2, ROWS, LANES),
            wide(2, ROWS, LANES),
            narrow(2 * ROWS, channels),
            narrow(2 * ROWS, 2 * STATE),
            narrow(2 * ROWS, 2 * STATE),
            narrow(2 * ROWS, LANES),
            narrow(2 * ROWS, LANES),
            wide(*send.shape),
            wide(2, layers, each, HEAD + 8, STATE),
            wide(2, layers, each, HEAD + 8, STATE),
            wide(2, layers, each, HEAD, STATE),
            wide(2, layers, each, HEAD, STATE),
            wide(2, ROW, channels, STATE),
            wide(2, ranks, ROWS, width),
            wide(2, ranks, ROWS, width),
            dma(5),
            dma(2, ROW),
            dma(2, ROW),
            dma(2, layers),
            dma(2, layers),
            dma(2, layers),
            dma(2, layers),
            dma(2, ROW),
            dma(2, ROW),
            dma(2, ranks),
            dma(2, ranks),
        ],
        far=5,
        collective_id=1,
        has_side_effects=True,
    )


def solution(mesh):
    rows = P(("dp", "seq"), None)
    tiles = P(("dp", "seq"), "chan")
    in_specs = (rows, rows, P(None, "chan"), P(), P(None, "chan"), P("chan"), P("chan"), P("chan"), tiles, tiles)
    return jax.shard_map(
        local, mesh=mesh, in_specs=in_specs, out_specs=(tiles,) * 4, check_vma=False
    )
```

```python
import functools

import jax
import jax.numpy as jnp
from jax import lax
from jax.experimental import pallas as pl
from jax.experimental.pallas import tpu as pltpu
from jax.sharding import PartitionSpec as P

F32 = jnp.float32
BF16 = jnp.bfloat16
HIGHEST = lax.Precision.HIGHEST
HEAD = 64
STATE = 128
ROWS = 128
FLIP = 256
LANES = 128
ROW = 4


def dot(a, b, ca=1, cb=0, precision=None):
    return lax.dot_general(
        a, b, (((ca,), (cb,)), ((), ())), precision=precision, preferred_element_type=F32
    )


def split(a):
    high = a.astype(BF16)
    return high, (a - high.astype(F32)).astype(BF16)


def dot_left(a, b, ca=1, cb=0):
    high, low = split(a)
    return dot(high, b, ca, cb) + dot(low, b, ca, cb)


def dot_right(a, b, ca=1, cb=0):
    high, low = split(b)
    return dot(a, high, ca, cb) + dot(a, low, ca, cb)


def dot_both(a, b, ca=1, cb=0):
    a_high, a_low = split(a)
    b_high, b_low = split(b)
    return dot(a_high, b_high, ca, cb) + (dot(a_high, b_low, ca, cb) + dot(a_low, b_high, ca, cb))


def iota(shape, dim):
    return lax.broadcasted_iota(jnp.int32, shape, dim)


def where01(mask, dtype=F32):
    return jnp.where(mask, 1.0, 0.0).astype(dtype)


def anti_identity():
    return where01(iota((FLIP, FLIP), 0) + iota((FLIP, FLIP), 1) == FLIP - 1, BF16)


def spread_matrix(channels):
    lanes = iota((LANES, channels), 1)
    row = iota((LANES, channels), 0) * HEAD
    return where01((lanes >= row) & (lanes < row + HEAD), BF16)


def decay_parts(dt, rate):
    log_decay = -dt * rate
    strict = where01(iota((ROWS, ROWS), 0) > iota((ROWS, ROWS), 1))
    before = dot(strict, log_decay, precision=HIGHEST)
    upto = before + log_decay
    total = upto[ROWS - 1 : ROWS, :]
    return log_decay, before, upto, total


def project(fetches, source, complement, inner, select, step, step_wide, params, values, keys, dts, sigs):
    fetch_complement, fetch_hidden, fetch_step, fetch_select, fetch_inner = fetches
    depth = complement.shape[1]
    blocks = depth // FLIP
    anti = anti_identity()
    fetch_complement.wait()
    for b in range(blocks):
        block = complement[:, (blocks - 1 - b) * FLIP : (blocks - b) * FLIP]
        source[ROWS:, b * FLIP : (b + 1) * FLIP] = dot(block, anti).astype(BF16)
    step_wide[...] = jnp.zeros_like(step_wide)
    fetch_step.wait()
    step_wide[: step.shape[0], :] = step[...]
    fetch_hidden.wait()
    src = source[...]
    raw = dot(src, step_wide[...], 1, 1) + params[0:1, :]
    fetch_select.wait()
    k_all = dot(src, select[...]).astype(BF16)
    fetch_inner.wait()
    v_all = dot(src, inner[...]).astype(BF16)
    small = jnp.exp(-jnp.abs(raw))
    one_more = 1.0 + small
    tail = jnp.where(
        one_more == 1.0, small, jnp.log(one_more) * (small / jnp.where(one_more == 1.0, 1.0, one_more - 1.0))
    )
    dt_all = jnp.maximum(raw, 0.0) + tail
    values[...] = v_all
    keys[...] = k_all
    dts[...] = dt_all
    sigs[...] = jnp.where(raw >= 0.0, 1.0, small) / one_more


def chunk_states(s, values, keys, dts, rate, g_b, send):
    channels = values.shape[1]
    heads = channels // HEAD
    spread = spread_matrix(channels)
    ones = jnp.ones((ROWS, STATE), F32)
    rows = slice(s * ROWS, (s + 1) * ROWS)
    dt = dts[rows, :]
    log_decay, before, upto, total = decay_parts(dt, rate)
    x = values[rows, :].astype(F32)
    g = g_b.astype(F32)
    write, read = keys[rows, :STATE], keys[rows, STATE:]
    widen = lambda w: dot_left(w, spread)
    pieces = (
        (0, 0, widen(jnp.exp(total - upto) * dt) * x, write),
        (0, 1, widen(jnp.exp(total - before)) * g, read),
        (1, 0, widen(jnp.exp(before) * dt) * x, write),
        (1, 1, widen(jnp.exp(upto)) * g, read),
    )
    for way, kind, left, right in pieces:
        state = dot_left(left, right, 0, 0)
        send[way * 2 + kind, s, :channels, :] = state
    decay = jnp.exp(dot(log_decay, ones, 0, 0, precision=HIGHEST))
    for q in range(ROW):
        for h in range(heads):
            at = channels + 8 * h
            send[q, s, at : at + 8, :] = jnp.broadcast_to(decay[h : h + 1], (8, STATE))


def within_chunk(s, values, keys, dts, rate, g_b, y_in, d_in, key_in, row_sums, column_sums):
    heads = values.shape[1] // HEAD
    row_id, col_id = iota((ROWS, ROWS), 0), iota((ROWS, ROWS), 1)
    diagonal, lower, upper = row_id == col_id, row_id > col_id, row_id < col_id
    eye = where01(diagonal)
    twice = jnp.where(diagonal, 2.0, 1.0)
    lane_first = where01(iota((1, 2 * HEAD), 1) < HEAD, BF16)
    lane_second = where01(iota((1, 2 * HEAD), 1) >= HEAD, BF16)
    head_lane = iota((ROWS, LANES), 1)
    rows = slice(s * ROWS, (s + 1) * ROWS)
    dt = dts[rows, :]
    log_decay, before, upto, total = decay_parts(dt, rate)
    dt_t = dot(dt, eye, 0, 0, precision=HIGHEST)
    before_t = dot(log_decay, where01(upper), 0, 0, precision=HIGHEST)
    upto_t = before_t + dot(log_decay, eye, 0, 0, precision=HIGHEST)
    write, read = keys[rows, :STATE], keys[rows, STATE:]
    scores = dot(read, write, 1, 1)
    d_scores = jnp.zeros((ROWS, ROWS), F32)
    by_row = jnp.zeros((ROWS, LANES), F32)
    by_row_up = jnp.zeros((ROWS, LANES), F32)
    for pair in range(heads // 2):
        lanes = slice(pair * 2 * HEAD, (pair + 1) * 2 * HEAD)
        x_pair, g_pair = values[rows, lanes], g_b[:, lanes]
        y_pair = jnp.zeros((ROWS, 2 * HEAD), F32)
        d_pair = jnp.zeros((ROWS, 2 * HEAD), F32)
        for half, lane_mask in ((0, lane_first), (1, lane_second)):
            h = pair * 2 + half
            x_h, g_h = x_pair * lane_mask, g_pair * lane_mask
            gap = jnp.where(
                upper,
                before_t[h : h + 1, :] - before[:, h : h + 1],
                upto[:, h : h + 1] - upto_t[h : h + 1, :],
            )
            decay = jnp.exp(jnp.minimum(gap, 0.0)) * twice
            dt_row = dt_t[h : h + 1, :]
            scaled = scores * decay
            w_high, w_low = split(scaled * dt_row)
            y_pair = y_pair + (dot(w_high, x_h) + dot(w_low, x_h))
            d_pair = d_pair + (dot(w_high, g_h, 0, 0) + dot(w_low, g_h, 0, 0))
            outer = dot(g_h, x_pair, 1, 1)
            grads = outer * scaled
            d_scores = d_scores + outer * (decay * dt_row)
            q = grads * dt_row
            q_low, q_up = jnp.where(lower, q, 0.0), jnp.where(upper, q, 0.0)
            by_row = jnp.where(head_lane == h, jnp.sum(q_low, 1, keepdims=True), by_row)
            by_row_up = jnp.where(head_lane == h, jnp.sum(q_up, 1, keepdims=True), by_row_up)
            column_sums[s, h : h + 1, :] = jnp.sum(grads, 0, keepdims=True)
            column_sums[s, heads + h : heads + h + 1, :] = jnp.sum(q_low, 0, keepdims=True)
            column_sums[s, 2 * heads + h : 2 * heads + h + 1, :] = jnp.sum(q_up, 0, keepdims=True)
        y_in[rows, lanes] = y_pair
        d_in[rows, lanes] = d_pair
    row_sums[s, 0] = by_row
    row_sums[s, 1] = by_row_up
    key_in[rows, :STATE] = dot_left(d_scores, read, 0, 0)
    key_in[rows, STATE:] = dot_left(d_scores, write)


def finish(
    s,
    entry,
    values,
    keys,
    dts,
    sigs,
    params,
    g_b,
    y_in,
    d_in,
    key_in,
    row_sums,
    column_sums,
    mixed,
    d_val,
    d_key_high,
    d_key_low,
    d_raw_high,
    d_raw_low,
):
    channels = values.shape[1]
    heads = channels // HEAD
    rate, skip = params[1:2, :], params[2:3, :]
    spread = spread_matrix(channels)
    row_id, col_id = iota((ROWS, ROWS), 0), iota((ROWS, ROWS), 1)
    widen = lambda w: dot_left(w, spread)
    narrow = lambda w: dot_left(w, spread, 1, 1)
    skip_wide = widen(skip)
    rows = slice(s * ROWS, (s + 1) * ROWS)
    dt = dts[rows, :]
    log_decay, before, upto, total = decay_parts(dt, rate)
    x, g = values[rows, :].astype(F32), g_b.astype(F32)
    write, read = keys[rows, :STATE], keys[rows, STATE:]
    u_fwd, u_bwd = widen(jnp.exp(total - upto)), widen(jnp.exp(before))
    w_fwd, w_bwd = widen(jnp.exp(upto)), widen(jnp.exp(total - before))
    dt_wide = widen(dt)
    h_in, m_in, k_in, l_in = entry[0, s], entry[1, s], entry[2, s], entry[3, s]
    y_fwd = w_fwd * dot_right(read, h_in, 1, 1)
    y_bwd = w_bwd * dot_right(read, k_in, 1, 1)
    x_l = u_fwd * dot_right(write, l_in, 1, 1)
    x_m = u_bwd * dot_right(write, m_in, 1, 1)
    d_read = dot_both(w_fwd * g, h_in) + dot_both(w_bwd * g, k_in)
    d_write = dot_both(u_fwd * dt_wide * x, l_in) + dot_both(u_bwd * dt_wide * x, m_in)
    r_fwd, r_bwd = narrow(g * y_fwd), narrow(g * y_bwd)
    q_fwd, q_bwd = narrow(x * x_l), narrow(x * x_m)
    both = dot_right(spread, l_in * h_in + m_in * k_in)
    both = dot(jnp.ones((8, STATE), F32), both, 1, 1, precision=HIGHEST)[0:1]
    out = y_in[rows, :] + y_fwd + y_bwd + skip_wide * x
    mixed[...] = out.astype(BF16)
    d_val[rows, :] = (d_in[rows, :] + dt_wide * (x_l + x_m) + skip_wide * g).astype(BF16)
    sums = column_sums[s]
    picked = lambda at: dot_left(sums, where01((row_id == col_id + at) & (col_id < heads), BF16), 0, 0)
    d_dt = picked(0) + q_fwd + q_bwd
    d_upto = row_sums[s, 0] - picked(heads) + r_fwd - dt * q_fwd
    d_before = picked(2 * heads) - row_sums[s, 1] - r_bwd + dt * q_bwd
    d_total = jnp.sum(r_bwd + dt * q_fwd, 0, keepdims=True) + jnp.exp(total) * both
    d_log = dot(where01(row_id <= col_id), d_upto, precision=HIGHEST)
    d_log = d_log + dot(where01(row_id < col_id), d_before, precision=HIGHEST) + d_total
    d_raw_high[rows, :], d_raw_low[rows, :] = split((d_dt - rate * d_log) * sigs[rows, :])
    d_key_high[rows, :STATE], d_key_low[rows, :STATE] = split(d_write + key_in[rows, :STATE])
    d_key_high[rows, STATE:], d_key_low[rows, STATE:] = split(d_read + key_in[rows, STATE:])


def main_kernel(
    layers,
    ranks,
    complement_hbm,
    hidden_hbm,
    step_hbm,
    select_hbm,
    inner_hbm,
    cot_hbm,
    ccot_hbm,
    params,
    mixed,
    cmixed,
    first,
    second,
    complement,
    source,
    send,
    values,
    keys,
    dts,
    sigs,
    cot,
    ccot,
    inner,
    select,
    step,
    step_wide,
    entry,
    y_in,
    d_in,
    key_in,
    row_sums,
    column_sums,
    d_val,
    d_key_high,
    d_key_low,
    d_raw_high,
    d_raw_low,
    rows_in,
    sums,
    layered,
    scanned,
    before,
    members,
    term,
    shares,
    sems,
    gather_out,
    gather_in,
    up_out,
    up_in,
    back_out,
    back_in,
    spread_out,
    spread_in,
    share_out,
    share_in,
):
    fetches = [
        pltpu.make_async_copy(here, there, sems.at[i])
        for i, (here, there) in enumerate(
            (
                (complement_hbm, complement),
                (hidden_hbm, source.at[:ROWS]),
                (step_hbm, step),
                (select_hbm, select),
                (inner_hbm, inner),
                (cot_hbm, cot),
                (ccot_hbm, ccot),
            )
        )
    ]
    for fetch in fetches:
        fetch.start()
    me, rank = lax.axis_index("seq"), lax.axis_index("chan")
    channels = values.shape[1]
    heads = channels // HEAD
    width = term.shape[3]
    layer, member = me // ROW, lax.rem(me, ROW)
    down = member // 2
    each = heads // layers
    side = lambda j: layer * ROW + lax.rem(member + j, ROW)
    over = lambda j: lax.rem(layer + j, layers) * ROW + member
    across = lambda j: lax.rem(rank + j, ranks)
    place = {"device_id_type": pl.DeviceIdType.MESH}
    barrier = pltpu.get_barrier_semaphore()
    for j in range(1, ROW):
        pl.semaphore_signal(barrier, inc=1, device_id={"seq": side(j)}, **place)
    for j in range(1, layers):
        pl.semaphore_signal(barrier, inc=1, device_id={"seq": over(j)}, **place)
    for j in range(1, ranks):
        pl.semaphore_signal(barrier, inc=1, device_id={"chan": across(j)}, **place)
    project(fetches[:5], source, complement, inner, select, step, step_wide, params, values, keys, dts, sigs)

    def copy(here, there, sent, got, device):
        return pltpu.make_async_remote_copy(
            src_ref=here, dst_ref=there, send_sem=sent, recv_sem=got, device_id=device, **place
        )

    def gather(half, j):
        peer = lax.rem(member + j, ROW)
        there = rows_in.at[member, half]
        return copy(send.at[peer, half], there, gather_out.at[half, j], gather_in.at[half, j], {"seq": side(j)})

    def up(half, j):
        peer = lax.rem(layer + j, layers)
        there = layered.at[half, layer]
        return copy(sums.at[half, peer], there, up_out.at[half, j], up_in.at[half, j], {"seq": over(j)})

    def give_back(half, j):
        peer = lax.rem(layer + j, layers)
        there = before.at[half, layer]
        return copy(scanned.at[half, peer], there, back_out.at[half, j], back_in.at[half, j], {"seq": over(j)})

    def spread(half, j):
        peer = lax.rem(member + j, ROW)
        there = entry.at[member, half]
        return copy(members.at[half, peer], there, spread_out.at[half, j], spread_in.at[half, j], {"seq": side(j)})

    def share(half, j):
        there = shares.at[half, rank]
        return copy(term.at[half, across(j)], there, share_out.at[half, j], share_in.at[half, j], {"chan": across(j)})

    order = (1, 3, 2)
    far = tuple(j for j in (1, 7, 2, 6, 3, 5, 4) if j < layers)
    for s, g in ((0, cot), (1, ccot)):
        fetches[5 + s].wait()
        chunk_states(s, values, keys, dts, params[1:2, :], g[...], send)
        if s == 0:
            pl.semaphore_wait(barrier, ROW + layers + ranks - 3)
        for j in order:
            gather(s, j).start()
    rows_in[member] = send[member]
    column_sums[...] = jnp.zeros_like(column_sums)
    for s, g in ((0, cot), (1, ccot)):
        within_chunk(s, values, keys, dts, params[1:2, :], g[...], y_in, d_in, key_in, row_sums, column_sums)
    zero = jnp.zeros((HEAD // 8, 8, STATE), F32)

    def part(source, h, half):
        return rows_in[source, half, pl.ds(pl.multiple_of(h * HEAD, 8), HEAD), :].reshape(HEAD // 8, 8, STATE)

    def decay(source, h, half):
        return rows_in[source, half, pl.ds(pl.multiple_of(channels + 8 * h, 8), 8), :]

    def turned(lap, count):
        return lap + down * (count - 1 - 2 * lap)

    for half in range(2):
        for j in order:
            gather(half, j).wait_recv()

        def total(h, carry):
            state = zero
            through = jnp.ones((8, STATE), F32)
            for m in range(ROW):
                source = turned(m, ROW)
                slower = decay(source, h, half)
                state = state * slower[None] + part(source, h, half)
                through = through * slower
            sums[half, h // each, h % each, :HEAD, :] = state.reshape(HEAD, STATE)
            sums[half, h // each, h % each, HEAD:, :] = through
            return carry

        lax.fori_loop(0, heads, total, 0)
        for j in far:
            up(half, j).start()
        layered[half, layer] = sums[half, layer]
        for j in far:
            up(half, j).wait_recv()
        for e in range(each):

            def scan(lap, state):
                at = turned(lap, layers)
                scanned[half, at, e] = state.reshape(HEAD, STATE)
                slower = layered[half, at, e, HEAD:, :]
                return state * slower[None] + layered[half, at, e, :HEAD, :].reshape(HEAD // 8, 8, STATE)

            lax.fori_loop(0, layers, scan, zero)
        for j in far:
            give_back(half, j).start()
        before[half, layer] = scanned[half, layer]
        for j in far:
            give_back(half, j).wait_recv()

        def unfold(h, carry):
            state = before[half, h // each, h % each].reshape(HEAD // 8, 8, STATE)
            for m in range(ROW):
                target = turned(m, ROW)
                members[half, target, pl.ds(pl.multiple_of(h * HEAD, 8), HEAD), :] = state.reshape(HEAD, STATE)
                if m < ROW - 1:
                    state = state * decay(target, h, half)[None] + part(target, h, half)
            return carry

        lax.fori_loop(0, heads, unfold, 0)
        for j in order:
            spread(half, j).start()
        entry[member, half] = members[half, member]

    def chunk(half, block):
        rows = slice(half * ROWS, (half + 1) * ROWS)
        cols = pl.ds(pl.multiple_of(block * width, width), width)
        value = dot(d_val[rows, :], inner[cols, :], 1, 1)
        picked = select[cols, :]
        value = value + (dot(d_key_high[rows, :], picked, 1, 1) + dot(d_key_low[rows, :], picked, 1, 1))
        steps = step_wide[:, cols]
        return value + (dot(d_raw_high[rows, :], steps) + dot(d_raw_low[rows, :], steps))

    for s, g, out in ((0, cot, mixed), (1, ccot, cmixed)):
        for j in order:
            spread(s, j).wait_recv()
        finish(
            s,
            entry,
            values,
            keys,
            dts,
            sigs,
            params,
            g[...],
            y_in,
            d_in,
            key_in,
            row_sums,
            column_sums,
            out,
            d_val,
            d_key_high,
            d_key_low,
            d_raw_high,
            d_raw_low,
        )
        for j in range(1, ranks + 1):
            peer = across(j)
            term[s, peer] = chunk(s, ranks - 1 - peer if s else peer)
            if j < ranks:
                share(s, j).start()
    anti = anti_identity()
    for s in range(2):
        result = term[s, rank]
        for j in range(1, ranks):
            share(s, j).wait_recv()
            result = result + shares[s, across(ranks - j)]
        result = result.astype(BF16)
        if s == 0:
            first[...] = result
        else:
            blocks = width // FLIP
            for b in range(blocks):
                block = result[:, (blocks - 1 - b) * FLIP : (blocks - b) * FLIP]
                second[:, b * FLIP : (b + 1) * FLIP] = dot(block, anti).astype(BF16)
    for half in range(2):
        for j in order:
            gather(half, j).wait_send()
            spread(half, j).wait_send()
        for j in far:
            up(half, j).wait_send()
            give_back(half, j).wait_send()
        for j in range(1, ranks):
            share(half, j).wait_send()


def call(kernel, outs, args, scratch=(), far=0, **params):
    whole = pl.BlockSpec(memory_space=pltpu.VMEM)
    return pl.pallas_call(
        kernel,
        out_shape=[jax.ShapeDtypeStruct(shape, dtype) for shape, dtype in outs],
        in_specs=[pl.BlockSpec(memory_space=pltpu.HBM)] * far + [whole] * (len(args) - far),
        out_specs=[whole] * len(outs),
        scratch_shapes=list(scratch),
        compiler_params=pltpu.CompilerParams(vmem_limit_bytes=48 << 20, **params),
    )(*[pltpu.with_memory_space_constraint(a, pltpu.HBM) for a in args[:far]], *args[far:])


def local(hidden, complement, inner, select, step, bias, rate, skip, cot, ccot):
    shards, ranks = lax.axis_size("seq"), lax.axis_size("chan")
    heads = bias.shape[0]
    depth = hidden.shape[1]
    channels = heads * HEAD
    params = jnp.pad(jnp.stack([bias, rate, skip]), ((0, 5), (0, LANES - heads)))
    step = step.T
    layers = shards // ROW
    each = heads // layers
    width = depth // ranks
    dma = lambda *count: pltpu.SemaphoreType.DMA(count)
    wide = lambda *shape: pltpu.VMEM(shape, F32)
    narrow = lambda *shape: pltpu.VMEM(shape, BF16)
    return call(
        functools.partial(main_kernel, layers, ranks),
        [((ROWS, channels), BF16)] * 2 + [((ROWS, width), BF16)] * 2,
        (complement, hidden, step, select, inner, cot, ccot, params),
        [
            narrow(ROWS, depth),
            narrow(2 * ROWS, depth),
            wide(ROW, 2, channels + 8 * heads, STATE),
            narrow(2 * ROWS, channels),
            narrow(2 * ROWS, 2 * STATE),
            wide(2 * ROWS, LANES),
            wide(2 * ROWS, LANES),
            narrow(*cot.shape),
            narrow(*ccot.shape),
            narrow(*inner.shape),
            narrow(*select.shape),
            narrow(*step.shape),
            narrow(LANES, depth),
            wide(ROW, 2, channels, STATE),
            wide(2 * ROWS, channels),
            wide(2 * ROWS, channels),
            wide(2 * ROWS, 2 * STATE),
            wide(2, 2, ROWS, LANES),
            wide(2, ROWS, LANES),
            narrow(2 * ROWS, channels),
            narrow(2 * ROWS, 2 * STATE),
            narrow(2 * ROWS, 2 * STATE),
            narrow(2 * ROWS, LANES),
            narrow(2 * ROWS, LANES),
            wide(ROW, 2, channels + 8 * heads, STATE),
            wide(2, layers, each, HEAD + 8, STATE),
            wide(2, layers, each, HEAD + 8, STATE),
            wide(2, layers, each, HEAD, STATE),
            wide(2, layers, each, HEAD, STATE),
            wide(2, ROW, channels, STATE),
            wide(2, ranks, ROWS, width),
            wide(2, ranks, ROWS, width),
            dma(7),
            dma(2, ROW),
            dma(2, ROW),
            dma(2, layers),
            dma(2, layers),
            dma(2, layers),
            dma(2, layers),
            dma(2, ROW),
            dma(2, ROW),
            dma(2, ranks),
            dma(2, ranks),
        ],
        far=7,
        collective_id=1,
        has_side_effects=True,
    )


def solution(mesh):
    rows = P(("dp", "seq"), None)
    tiles = P(("dp", "seq"), "chan")
    in_specs = (rows, rows, P(None, "chan"), P(), P(None, "chan"), P("chan"), P("chan"), P("chan"), tiles, tiles)
    return jax.shard_map(
        local, mesh=mesh, in_specs=in_specs, out_specs=(tiles,) * 4, check_vma=False
    )
```

```python
import functools

import jax
import jax.numpy as jnp
from jax import lax
from jax.experimental import pallas as pl
from jax.experimental.pallas import tpu as pltpu
from jax.sharding import PartitionSpec as P

F32 = jnp.float32
BF16 = jnp.bfloat16
HIGHEST = lax.Precision.HIGHEST
HEAD = 64
STATE = 128
ROWS = 128
FLIP = 256
LANES = 128
ROW = 4


def dot(a, b, ca=1, cb=0, precision=None):
    return lax.dot_general(
        a, b, (((ca,), (cb,)), ((), ())), precision=precision, preferred_element_type=F32
    )


def split(a):
    high = a.astype(BF16)
    return high, (a - high.astype(F32)).astype(BF16)


def dot_left(a, b, ca=1, cb=0):
    high, low = split(a)
    return dot(high, b, ca, cb) + dot(low, b, ca, cb)


def dot_right(a, b, ca=1, cb=0):
    high, low = split(b)
    return dot(a, high, ca, cb) + dot(a, low, ca, cb)


def dot_terms(a, b, ca=1, cb=0):
    a_high, a_low = a
    b_high, b_low = split(b)
    return dot(a_high, b_high, ca, cb) + (dot(a_high, b_low, ca, cb) + dot(a_low, b_high, ca, cb))


def iota(shape, dim):
    return lax.broadcasted_iota(jnp.int32, shape, dim)


def where01(mask, dtype=F32):
    return jnp.where(mask, 1.0, 0.0).astype(dtype)


def anti_identity():
    return where01(iota((FLIP, FLIP), 0) + iota((FLIP, FLIP), 1) == FLIP - 1, BF16)


def spread_matrix(channels):
    lanes = iota((LANES, channels), 1)
    row = iota((LANES, channels), 0) * HEAD
    return where01((lanes >= row) & (lanes < row + HEAD), BF16)


def decay_parts(dt, rate):
    log_decay = -dt * rate
    strict = where01(iota((ROWS, ROWS), 0) > iota((ROWS, ROWS), 1))
    before = dot(strict, log_decay, precision=HIGHEST)
    upto = before + log_decay
    total = upto[ROWS - 1 : ROWS, :]
    return log_decay, before, upto, total


def project(fetches, source, complement, inner, select, step, step_wide, params, values, keys, dts, sigs):
    fetch_complement, fetch_hidden, fetch_step, fetch_select, fetch_inner = fetches
    depth = complement.shape[1]
    blocks = depth // FLIP
    anti = anti_identity()
    fetch_complement.wait()
    for b in range(blocks):
        block = complement[:, (blocks - 1 - b) * FLIP : (blocks - b) * FLIP]
        source[ROWS:, b * FLIP : (b + 1) * FLIP] = dot(block, anti).astype(BF16)
    step_wide[...] = jnp.zeros_like(step_wide)
    fetch_step.wait()
    step_wide[: step.shape[0], :] = step[...]
    fetch_hidden.wait()
    src = source[...]
    raw = dot(src, step_wide[...], 1, 1) + params[0:1, :]
    fetch_select.wait()
    k_all = dot(src, select[...]).astype(BF16)
    fetch_inner.wait()
    v_all = dot(src, inner[...]).astype(BF16)
    small = jnp.exp(-jnp.abs(raw))
    one_more = 1.0 + small
    tail = jnp.where(
        one_more == 1.0, small, jnp.log(one_more) * (small / jnp.where(one_more == 1.0, 1.0, one_more - 1.0))
    )
    dt_all = jnp.maximum(raw, 0.0) + tail
    values[...] = v_all
    keys[...] = k_all
    dts[...] = dt_all
    sigs[...] = jnp.where(raw >= 0.0, 1.0, small) / one_more


def chunk_states(s, values, keys, dts, rate, g_b, send):
    channels = values.shape[1]
    heads = channels // HEAD
    spread = spread_matrix(channels)
    ones = jnp.ones((ROWS, STATE), F32)
    rows = slice(s * ROWS, (s + 1) * ROWS)
    dt = dts[rows, :]
    log_decay, before, upto, total = decay_parts(dt, rate)
    x = values[rows, :].astype(F32)
    g = g_b.astype(F32)
    write, read = keys[rows, :STATE], keys[rows, STATE:]
    widen = lambda w: dot_left(w, spread)
    pieces = (
        (0, 0, widen(jnp.exp(total - upto) * dt) * x, write),
        (0, 1, widen(jnp.exp(total - before)) * g, read),
        (1, 0, widen(jnp.exp(before) * dt) * x, write),
        (1, 1, widen(jnp.exp(upto)) * g, read),
    )
    for way, kind, left, right in pieces:
        state = dot_left(left, right, 0, 0)
        send[way * 2 + kind, s, :channels, :] = state
    decay = jnp.exp(dot(log_decay, ones, 0, 0, precision=HIGHEST))
    for q in range(ROW):
        for h in range(heads):
            at = channels + 8 * h
            send[q, s, at : at + 8, :] = jnp.broadcast_to(decay[h : h + 1], (8, STATE))


def within_chunk(s, values, keys, dts, rate, g_b, y_in, d_in, key_in, row_sums, column_sums):
    heads = values.shape[1] // HEAD
    row_id, col_id = iota((ROWS, ROWS), 0), iota((ROWS, ROWS), 1)
    diagonal, lower, upper = row_id == col_id, row_id > col_id, row_id < col_id
    eye = where01(diagonal)
    twice = jnp.where(diagonal, 2.0, 1.0)
    lane_first = where01(iota((1, 2 * HEAD), 1) < HEAD, BF16)
    lane_second = where01(iota((1, 2 * HEAD), 1) >= HEAD, BF16)
    head_lane = iota((ROWS, LANES), 1)
    rows = slice(s * ROWS, (s + 1) * ROWS)
    dt = dts[rows, :]
    log_decay, before, upto, total = decay_parts(dt, rate)
    dt_t = dot(dt, eye, 0, 0, precision=HIGHEST)
    before_t = dot(log_decay, where01(upper), 0, 0, precision=HIGHEST)
    upto_t = before_t + dot(log_decay, eye, 0, 0, precision=HIGHEST)
    write, read = keys[rows, :STATE], keys[rows, STATE:]
    scores = dot(read, write, 1, 1)
    d_scores = jnp.zeros((ROWS, ROWS), F32)
    by_row = jnp.zeros((ROWS, LANES), F32)
    by_row_up = jnp.zeros((ROWS, LANES), F32)
    for pair in range(heads // 2):
        lanes = slice(pair * 2 * HEAD, (pair + 1) * 2 * HEAD)
        x_pair, g_pair = values[rows, lanes], g_b[:, lanes]
        y_pair = jnp.zeros((ROWS, 2 * HEAD), F32)
        d_pair = jnp.zeros((ROWS, 2 * HEAD), F32)
        for half, lane_mask in ((0, lane_first), (1, lane_second)):
            h = pair * 2 + half
            x_h, g_h = x_pair * lane_mask, g_pair * lane_mask
            gap = jnp.where(
                upper,
                before_t[h : h + 1, :] - before[:, h : h + 1],
                upto[:, h : h + 1] - upto_t[h : h + 1, :],
            )
            decay = jnp.exp(jnp.minimum(gap, 0.0)) * twice
            dt_row = dt_t[h : h + 1, :]
            scaled = scores * decay
            w_high, w_low = split(scaled * dt_row)
            y_pair = y_pair + (dot(w_high, x_h) + dot(w_low, x_h))
            d_pair = d_pair + (dot(w_high, g_h, 0, 0) + dot(w_low, g_h, 0, 0))
            outer = dot(g_h, x_pair, 1, 1)
            grads = outer * scaled
            d_scores = d_scores + outer * (decay * dt_row)
            q = grads * dt_row
            q_low, q_up = jnp.where(lower, q, 0.0), jnp.where(upper, q, 0.0)
            by_row = jnp.where(head_lane == h, jnp.sum(q_low, 1, keepdims=True), by_row)
            by_row_up = jnp.where(head_lane == h, jnp.sum(q_up, 1, keepdims=True), by_row_up)
            column_sums[s, h : h + 1, :] = jnp.sum(grads, 0, keepdims=True)
            column_sums[s, heads + h : heads + h + 1, :] = jnp.sum(q_low, 0, keepdims=True)
            column_sums[s, 2 * heads + h : 2 * heads + h + 1, :] = jnp.sum(q_up, 0, keepdims=True)
        y_in[rows, lanes] = y_pair
        d_in[rows, lanes] = d_pair
    row_sums[s, 0] = by_row
    row_sums[s, 1] = by_row_up
    key_in[rows, :STATE] = dot_left(d_scores, read, 0, 0)
    key_in[rows, STATE:] = dot_left(d_scores, write)


def finish(
    s,
    wait,
    entry,
    values,
    keys,
    dts,
    sigs,
    params,
    g_b,
    y_in,
    d_in,
    key_in,
    row_sums,
    column_sums,
    mixed,
    d_val,
    d_key_high,
    d_key_low,
    d_raw_high,
    d_raw_low,
):
    channels = values.shape[1]
    heads = channels // HEAD
    rate, skip = params[1:2, :], params[2:3, :]
    spread = spread_matrix(channels)
    row_id, col_id = iota((ROWS, ROWS), 0), iota((ROWS, ROWS), 1)
    widen = lambda w: dot_left(w, spread)
    narrow = lambda w: dot_left(w, spread, 1, 1)
    skip_wide = widen(skip)
    rows = slice(s * ROWS, (s + 1) * ROWS)
    dt = dts[rows, :]
    log_decay, before, upto, total = decay_parts(dt, rate)
    x, g = values[rows, :].astype(F32), g_b.astype(F32)
    write, read = keys[rows, :STATE], keys[rows, STATE:]
    u_fwd, u_bwd = widen(jnp.exp(total - upto)), widen(jnp.exp(before))
    w_fwd, w_bwd = widen(jnp.exp(upto)), widen(jnp.exp(total - before))
    dt_wide = widen(dt)
    w_g_fwd, w_g_bwd = split(w_fwd * g), split(w_bwd * g)
    u_x_fwd, u_x_bwd = split(u_fwd * dt_wide * x), split(u_bwd * dt_wide * x)
    wait()
    h_in, m_in, k_in, l_in = entry[0, s], entry[1, s], entry[2, s], entry[3, s]
    y_fwd = w_fwd * dot_right(read, h_in, 1, 1)
    y_bwd = w_bwd * dot_right(read, k_in, 1, 1)
    x_l = u_fwd * dot_right(write, l_in, 1, 1)
    x_m = u_bwd * dot_right(write, m_in, 1, 1)
    d_read = dot_terms(w_g_fwd, h_in) + dot_terms(w_g_bwd, k_in)
    d_write = dot_terms(u_x_fwd, l_in) + dot_terms(u_x_bwd, m_in)
    r_fwd, r_bwd = narrow(g * y_fwd), narrow(g * y_bwd)
    q_fwd, q_bwd = narrow(x * x_l), narrow(x * x_m)
    both = dot_right(spread, l_in * h_in + m_in * k_in)
    both = dot(jnp.ones((8, STATE), F32), both, 1, 1, precision=HIGHEST)[0:1]
    out = y_in[rows, :] + y_fwd + y_bwd + skip_wide * x
    mixed[...] = out.astype(BF16)
    d_val[rows, :] = (d_in[rows, :] + dt_wide * (x_l + x_m) + skip_wide * g).astype(BF16)
    sums = column_sums[s]
    picked = lambda at: dot_left(sums, where01((row_id == col_id + at) & (col_id < heads), BF16), 0, 0)
    d_dt = picked(0) + q_fwd + q_bwd
    d_upto = row_sums[s, 0] - picked(heads) + r_fwd - dt * q_fwd
    d_before = picked(2 * heads) - row_sums[s, 1] - r_bwd + dt * q_bwd
    d_total = jnp.sum(r_bwd + dt * q_fwd, 0, keepdims=True) + jnp.exp(total) * both
    d_log = dot(where01(row_id <= col_id), d_upto, precision=HIGHEST)
    d_log = d_log + dot(where01(row_id < col_id), d_before, precision=HIGHEST) + d_total
    d_raw_high[rows, :], d_raw_low[rows, :] = split((d_dt - rate * d_log) * sigs[rows, :])
    d_key_high[rows, :STATE], d_key_low[rows, :STATE] = split(d_write + key_in[rows, :STATE])
    d_key_high[rows, STATE:], d_key_low[rows, STATE:] = split(d_read + key_in[rows, STATE:])


def main_kernel(
    layers,
    ranks,
    complement_hbm,
    hidden_hbm,
    step_hbm,
    select_hbm,
    inner_hbm,
    cot_hbm,
    ccot_hbm,
    params,
    mixed,
    cmixed,
    first,
    second,
    complement,
    source,
    send,
    values,
    keys,
    dts,
    sigs,
    cot,
    ccot,
    inner,
    select,
    step,
    step_wide,
    entry,
    y_in,
    d_in,
    key_in,
    row_sums,
    column_sums,
    d_val,
    d_key_high,
    d_key_low,
    d_raw_high,
    d_raw_low,
    rows_in,
    sums,
    layered,
    scanned,
    before,
    members,
    term,
    shares,
    sems,
    gather_out,
    gather_in,
    up_out,
    up_in,
    back_out,
    back_in,
    spread_out,
    spread_in,
    share_out,
    share_in,
):
    fetches = [
        pltpu.make_async_copy(here, there, sems.at[i])
        for i, (here, there) in enumerate(
            (
                (complement_hbm, complement),
                (hidden_hbm, source.at[:ROWS]),
                (step_hbm, step),
                (select_hbm, select),
                (inner_hbm, inner),
                (cot_hbm, cot),
                (ccot_hbm, ccot),
            )
        )
    ]
    for fetch in fetches:
        fetch.start()
    me, rank = lax.axis_index("seq"), lax.axis_index("chan")
    channels = values.shape[1]
    heads = channels // HEAD
    width = term.shape[3]
    layer, member = me // ROW, lax.rem(me, ROW)
    down = member // 2
    each = heads // layers
    side = lambda j: layer * ROW + lax.rem(member + j, ROW)
    over = lambda j: lax.rem(layer + j, layers) * ROW + member
    across = lambda j: lax.rem(rank + j, ranks)
    place = {"device_id_type": pl.DeviceIdType.MESH}
    barrier = pltpu.get_barrier_semaphore()
    for j in range(1, ROW):
        pl.semaphore_signal(barrier, inc=1, device_id={"seq": side(j)}, **place)
    for j in range(1, layers):
        pl.semaphore_signal(barrier, inc=1, device_id={"seq": over(j)}, **place)
    for j in range(1, ranks):
        pl.semaphore_signal(barrier, inc=1, device_id={"chan": across(j)}, **place)
    project(fetches[:5], source, complement, inner, select, step, step_wide, params, values, keys, dts, sigs)

    def copy(here, there, sent, got, device):
        return pltpu.make_async_remote_copy(
            src_ref=here, dst_ref=there, send_sem=sent, recv_sem=got, device_id=device, **place
        )

    def gather(half, j):
        peer = lax.rem(member + j, ROW)
        there = rows_in.at[member, half]
        return copy(send.at[peer, half], there, gather_out.at[half, j], gather_in.at[half, j], {"seq": side(j)})

    def up(half, j):
        peer = lax.rem(layer + j, layers)
        there = layered.at[half, layer]
        return copy(sums.at[half, peer], there, up_out.at[half, j], up_in.at[half, j], {"seq": over(j)})

    def give_back(half, j):
        peer = lax.rem(layer + j, layers)
        there = before.at[half, layer]
        return copy(scanned.at[half, peer], there, back_out.at[half, j], back_in.at[half, j], {"seq": over(j)})

    def spread(half, j):
        peer = lax.rem(member + j, ROW)
        there = entry.at[member, half]
        return copy(members.at[half, peer], there, spread_out.at[half, j], spread_in.at[half, j], {"seq": side(j)})

    def share(half, j):
        there = shares.at[half, rank]
        return copy(term.at[half, across(j)], there, share_out.at[half, j], share_in.at[half, j], {"chan": across(j)})

    order = (1, 3, 2)
    far = tuple(j for j in (1, 7, 2, 6, 3, 5, 4) if j < layers)
    for s, g in ((0, cot), (1, ccot)):
        fetches[5 + s].wait()
        chunk_states(s, values, keys, dts, params[1:2, :], g[...], send)
        if s == 0:
            pl.semaphore_wait(barrier, ROW + layers + ranks - 3)
        for j in order:
            gather(s, j).start()
    rows_in[member] = send[member]
    column_sums[...] = jnp.zeros_like(column_sums)
    for s, g in ((0, cot), (1, ccot)):
        within_chunk(s, values, keys, dts, params[1:2, :], g[...], y_in, d_in, key_in, row_sums, column_sums)
    zero = jnp.zeros((HEAD // 8, 8, STATE), F32)

    def part(source, h, half):
        return rows_in[source, half, pl.ds(pl.multiple_of(h * HEAD, 8), HEAD), :].reshape(HEAD // 8, 8, STATE)

    def decay(source, h, half):
        return rows_in[source, half, pl.ds(pl.multiple_of(channels + 8 * h, 8), 8), :]

    def turned(lap, count):
        return lap + down * (count - 1 - 2 * lap)

    for half in range(2):
        for j in order:
            gather(half, j).wait_recv()

        def total(h, carry):
            state = zero
            through = jnp.ones((8, STATE), F32)
            for m in range(ROW):
                source = turned(m, ROW)
                slower = decay(source, h, half)
                state = state * slower[None] + part(source, h, half)
                through = through * slower
            sums[half, h // each, h % each, :HEAD, :] = state.reshape(HEAD, STATE)
            sums[half, h // each, h % each, HEAD:, :] = through
            return carry

        lax.fori_loop(0, heads, total, 0)
        for j in far:
            up(half, j).start()
        layered[half, layer] = sums[half, layer]
        for j in far:
            up(half, j).wait_recv()
        for e in range(each):

            def scan(lap, state):
                at = turned(lap, layers)
                scanned[half, at, e] = state.reshape(HEAD, STATE)
                slower = layered[half, at, e, HEAD:, :]
                return state * slower[None] + layered[half, at, e, :HEAD, :].reshape(HEAD // 8, 8, STATE)

            lax.fori_loop(0, layers, scan, zero)
        for j in far:
            give_back(half, j).start()
        before[half, layer] = scanned[half, layer]
        for j in far:
            give_back(half, j).wait_recv()

        def unfold(h, carry):
            state = before[half, h // each, h % each].reshape(HEAD // 8, 8, STATE)
            for m in range(ROW):
                target = turned(m, ROW)
                members[half, target, pl.ds(pl.multiple_of(h * HEAD, 8), HEAD), :] = state.reshape(HEAD, STATE)
                if m < ROW - 1:
                    state = state * decay(target, h, half)[None] + part(target, h, half)
            return carry

        lax.fori_loop(0, heads, unfold, 0)
        for j in order:
            spread(half, j).start()
        entry[member, half] = members[half, member]

    def chunk(half, block):
        rows = slice(half * ROWS, (half + 1) * ROWS)
        cols = pl.ds(pl.multiple_of(block * width, width), width)
        value = dot(d_val[rows, :], inner[cols, :], 1, 1)
        picked = select[cols, :]
        value = value + (dot(d_key_high[rows, :], picked, 1, 1) + dot(d_key_low[rows, :], picked, 1, 1))
        steps = step_wide[:, cols]
        return value + (dot(d_raw_high[rows, :], steps) + dot(d_raw_low[rows, :], steps))

    for s, g, out in ((0, cot, mixed), (1, ccot, cmixed)):

        def settled():
            for j in order:
                spread(s, j).wait_recv()

        finish(
            s,
            settled,
            entry,
            values,
            keys,
            dts,
            sigs,
            params,
            g[...],
            y_in,
            d_in,
            key_in,
            row_sums,
            column_sums,
            out,
            d_val,
            d_key_high,
            d_key_low,
            d_raw_high,
            d_raw_low,
        )
        for j in range(1, ranks + 1):
            peer = across(j)
            term[s, peer] = chunk(s, ranks - 1 - peer if s else peer)
            if j < ranks:
                share(s, j).start()
    anti = anti_identity()
    for s in range(2):
        result = term[s, rank]
        for j in range(1, ranks):
            share(s, j).wait_recv()
            result = result + shares[s, across(ranks - j)]
        result = result.astype(BF16)
        if s == 0:
            first[...] = result
        else:
            blocks = width // FLIP
            for b in range(blocks):
                block = result[:, (blocks - 1 - b) * FLIP : (blocks - b) * FLIP]
                second[:, b * FLIP : (b + 1) * FLIP] = dot(block, anti).astype(BF16)
    for half in range(2):
        for j in order:
            gather(half, j).wait_send()
            spread(half, j).wait_send()
        for j in far:
            up(half, j).wait_send()
            give_back(half, j).wait_send()
        for j in range(1, ranks):
            share(half, j).wait_send()


def call(kernel, outs, args, scratch=(), far=0, **params):
    whole = pl.BlockSpec(memory_space=pltpu.VMEM)
    return pl.pallas_call(
        kernel,
        out_shape=[jax.ShapeDtypeStruct(shape, dtype) for shape, dtype in outs],
        in_specs=[pl.BlockSpec(memory_space=pltpu.HBM)] * far + [whole] * (len(args) - far),
        out_specs=[whole] * len(outs),
        scratch_shapes=list(scratch),
        compiler_params=pltpu.CompilerParams(vmem_limit_bytes=48 << 20, **params),
    )(*[pltpu.with_memory_space_constraint(a, pltpu.HBM) for a in args[:far]], *args[far:])


def local(hidden, complement, inner, select, step, bias, rate, skip, cot, ccot):
    shards, ranks = lax.axis_size("seq"), lax.axis_size("chan")
    heads = bias.shape[0]
    depth = hidden.shape[1]
    channels = heads * HEAD
    params = jnp.pad(jnp.stack([bias, rate, skip]), ((0, 5), (0, LANES - heads)))
    step = step.T
    layers = shards // ROW
    each = heads // layers
    width = depth // ranks
    dma = lambda *count: pltpu.SemaphoreType.DMA(count)
    wide = lambda *shape: pltpu.VMEM(shape, F32)
    narrow = lambda *shape: pltpu.VMEM(shape, BF16)
    return call(
        functools.partial(main_kernel, layers, ranks),
        [((ROWS, channels), BF16)] * 2 + [((ROWS, width), BF16)] * 2,
        (complement, hidden, step, select, inner, cot, ccot, params),
        [
            narrow(ROWS, depth),
            narrow(2 * ROWS, depth),
            wide(ROW, 2, channels + 8 * heads, STATE),
            narrow(2 * ROWS, channels),
            narrow(2 * ROWS, 2 * STATE),
            wide(2 * ROWS, LANES),
            wide(2 * ROWS, LANES),
            narrow(*cot.shape),
            narrow(*ccot.shape),
            narrow(*inner.shape),
            narrow(*select.shape),
            narrow(*step.shape),
            narrow(LANES, depth),
            wide(ROW, 2, channels, STATE),
            wide(2 * ROWS, channels),
            wide(2 * ROWS, channels),
            wide(2 * ROWS, 2 * STATE),
            wide(2, 2, ROWS, LANES),
            wide(2, ROWS, LANES),
            narrow(2 * ROWS, channels),
            narrow(2 * ROWS, 2 * STATE),
            narrow(2 * ROWS, 2 * STATE),
            narrow(2 * ROWS, LANES),
            narrow(2 * ROWS, LANES),
            wide(ROW, 2, channels + 8 * heads, STATE),
            wide(2, layers, each, HEAD + 8, STATE),
            wide(2, layers, each, HEAD + 8, STATE),
            wide(2, layers, each, HEAD, STATE),
            wide(2, layers, each, HEAD, STATE),
            wide(2, ROW, channels, STATE),
            wide(2, ranks, ROWS, width),
            wide(2, ranks, ROWS, width),
            dma(7),
            dma(2, ROW),
            dma(2, ROW),
            dma(2, layers),
            dma(2, layers),
            dma(2, layers),
            dma(2, layers),
            dma(2, ROW),
            dma(2, ROW),
            dma(2, ranks),
            dma(2, ranks),
        ],
        far=7,
        collective_id=1,
        has_side_effects=True,
    )


def solution(mesh):
    rows = P(("dp", "seq"), None)
    tiles = P(("dp", "seq"), "chan")
    in_specs = (rows, rows, P(None, "chan"), P(), P(None, "chan"), P("chan"), P("chan"), P("chan"), tiles, tiles)
    return jax.shard_map(
        local, mesh=mesh, in_specs=in_specs, out_specs=(tiles,) * 4, check_vma=False
    )
```

```python
import functools

import jax
import jax.numpy as jnp
from jax import lax
from jax.experimental import pallas as pl
from jax.experimental.pallas import tpu as pltpu
from jax.sharding import PartitionSpec as P

F32 = jnp.float32
BF16 = jnp.bfloat16
HIGHEST = lax.Precision.HIGHEST
HEAD = 64
STATE = 128
ROWS = 128
FLIP = 256
LANES = 128
ROW = 4


def dot(a, b, ca=1, cb=0, precision=None):
    return lax.dot_general(
        a, b, (((ca,), (cb,)), ((), ())), precision=precision, preferred_element_type=F32
    )


def split(a):
    high = a.astype(BF16)
    return high, (a - high.astype(F32)).astype(BF16)


def dot_left(a, b, ca=1, cb=0):
    high, low = split(a)
    return dot(high, b, ca, cb) + dot(low, b, ca, cb)


def dot_right(a, b, ca=1, cb=0):
    high, low = split(b)
    return dot(a, high, ca, cb) + dot(a, low, ca, cb)


def dot_both(a, b, ca=1, cb=0):
    a_high, a_low = split(a)
    b_high, b_low = split(b)
    return dot(a_high, b_high, ca, cb) + (dot(a_high, b_low, ca, cb) + dot(a_low, b_high, ca, cb))


def iota(shape, dim):
    return lax.broadcasted_iota(jnp.int32, shape, dim)


def where01(mask, dtype=F32):
    return jnp.where(mask, 1.0, 0.0).astype(dtype)


def anti_identity():
    return where01(iota((FLIP, FLIP), 0) + iota((FLIP, FLIP), 1) == FLIP - 1, BF16)


def spread_matrix(channels):
    lanes = iota((LANES, channels), 1)
    row = iota((LANES, channels), 0) * HEAD
    return where01((lanes >= row) & (lanes < row + HEAD), BF16)


def decay_parts(dt, rate):
    log_decay = -dt * rate
    strict = where01(iota((ROWS, ROWS), 0) > iota((ROWS, ROWS), 1))
    before = dot(strict, log_decay, precision=HIGHEST)
    upto = before + log_decay
    total = upto[ROWS - 1 : ROWS, :]
    return log_decay, before, upto, total


def project(fetches, source, complement, inner, select, step, step_wide, params, values, keys, dts, sigs):
    fetch_complement, fetch_hidden, fetch_step, fetch_select, fetch_inner = fetches
    depth = complement.shape[1]
    blocks = depth // FLIP
    anti = anti_identity()
    fetch_complement.wait()
    for b in range(blocks):
        block = complement[:, (blocks - 1 - b) * FLIP : (blocks - b) * FLIP]
        source[ROWS:, b * FLIP : (b + 1) * FLIP] = dot(block, anti).astype(BF16)
    step_wide[...] = jnp.zeros_like(step_wide)
    fetch_step.wait()
    step_wide[: step.shape[0], :] = step[...]
    fetch_hidden.wait()
    src = source[...]
    raw = dot(src, step_wide[...], 1, 1) + params[0:1, :]
    fetch_select.wait()
    k_all = dot(src, select[...]).astype(BF16)
    fetch_inner.wait()
    v_all = dot(src, inner[...]).astype(BF16)
    small = jnp.exp(-jnp.abs(raw))
    one_more = 1.0 + small
    tail = jnp.where(
        one_more == 1.0, small, jnp.log(one_more) * (small / jnp.where(one_more == 1.0, 1.0, one_more - 1.0))
    )
    dt_all = jnp.maximum(raw, 0.0) + tail
    values[...] = v_all
    keys[...] = k_all
    dts[...] = dt_all
    sigs[...] = jnp.where(raw >= 0.0, 1.0, small) / one_more


def chunk_states(s, values, keys, dts, rate, g_b, send):
    channels = values.shape[1]
    heads = channels // HEAD
    spread = spread_matrix(channels)
    ones = jnp.ones((ROWS, STATE), F32)
    rows = slice(s * ROWS, (s + 1) * ROWS)
    dt = dts[rows, :]
    log_decay, before, upto, total = decay_parts(dt, rate)
    x = values[rows, :].astype(F32)
    g = g_b.astype(F32)
    write, read = keys[rows, :STATE], keys[rows, STATE:]
    widen = lambda w: dot_left(w, spread)
    pieces = (
        (0, 0, widen(jnp.exp(total - upto) * dt) * x, write),
        (0, 1, widen(jnp.exp(total - before)) * g, read),
        (1, 0, widen(jnp.exp(before) * dt) * x, write),
        (1, 1, widen(jnp.exp(upto)) * g, read),
    )
    for way, kind, left, right in pieces:
        state = dot_left(left, right, 0, 0)
        send[way * 2 + kind, s, :channels, :] = state
    decay = jnp.exp(dot(log_decay, ones, 0, 0, precision=HIGHEST))
    for q in range(ROW):
        for h in range(heads):
            at = channels + 8 * h
            send[q, s, at : at + 8, :] = jnp.broadcast_to(decay[h : h + 1], (8, STATE))


def within_chunk(s, values, keys, dts, rate, g_b, y_in, d_in, key_in, row_sums, column_sums):
    heads = values.shape[1] // HEAD
    row_id, col_id = iota((ROWS, ROWS), 0), iota((ROWS, ROWS), 1)
    diagonal, lower, upper = row_id == col_id, row_id > col_id, row_id < col_id
    eye = where01(diagonal)
    twice = jnp.where(diagonal, 2.0, 1.0)
    lane_first = where01(iota((1, 2 * HEAD), 1) < HEAD, BF16)
    lane_second = where01(iota((1, 2 * HEAD), 1) >= HEAD, BF16)
    head_lane = iota((ROWS, LANES), 1)
    rows = slice(s * ROWS, (s + 1) * ROWS)
    dt = dts[rows, :]
    log_decay, before, upto, total = decay_parts(dt, rate)
    dt_t = dot(dt, eye, 0, 0, precision=HIGHEST)
    before_t = dot(log_decay, where01(upper), 0, 0, precision=HIGHEST)
    upto_t = before_t + dot(log_decay, eye, 0, 0, precision=HIGHEST)
    write, read = keys[rows, :STATE], keys[rows, STATE:]
    scores = dot(read, write, 1, 1)
    d_scores = jnp.zeros((ROWS, ROWS), F32)
    by_row = jnp.zeros((ROWS, LANES), F32)
    by_row_up = jnp.zeros((ROWS, LANES), F32)
    for pair in range(heads // 2):
        lanes = slice(pair * 2 * HEAD, (pair + 1) * 2 * HEAD)
        x_pair, g_pair = values[rows, lanes], g_b[:, lanes]
        y_pair = jnp.zeros((ROWS, 2 * HEAD), F32)
        d_pair = jnp.zeros((ROWS, 2 * HEAD), F32)
        for half, lane_mask in ((0, lane_first), (1, lane_second)):
            h = pair * 2 + half
            x_h, g_h = x_pair * lane_mask, g_pair * lane_mask
            gap = jnp.where(
                upper,
                before_t[h : h + 1, :] - before[:, h : h + 1],
                upto[:, h : h + 1] - upto_t[h : h + 1, :],
            )
            decay = jnp.exp(jnp.minimum(gap, 0.0)) * twice
            dt_row = dt_t[h : h + 1, :]
            scaled = scores * decay
            w_high, w_low = split(scaled * dt_row)
            y_pair = y_pair + (dot(w_high, x_h) + dot(w_low, x_h))
            d_pair = d_pair + (dot(w_high, g_h, 0, 0) + dot(w_low, g_h, 0, 0))
            outer = dot(g_h, x_pair, 1, 1)
            grads = outer * scaled
            d_scores = d_scores + outer * (decay * dt_row)
            q = grads * dt_row
            q_low, q_up = jnp.where(lower, q, 0.0), jnp.where(upper, q, 0.0)
            by_row = jnp.where(head_lane == h, jnp.sum(q_low, 1, keepdims=True), by_row)
            by_row_up = jnp.where(head_lane == h, jnp.sum(q_up, 1, keepdims=True), by_row_up)
            column_sums[s, h : h + 1, :] = jnp.sum(grads, 0, keepdims=True)
            column_sums[s, heads + h : heads + h + 1, :] = jnp.sum(q_low, 0, keepdims=True)
            column_sums[s, 2 * heads + h : 2 * heads + h + 1, :] = jnp.sum(q_up, 0, keepdims=True)
        y_in[rows, lanes] = y_pair
        d_in[rows, lanes] = d_pair
    row_sums[s, 0] = by_row
    row_sums[s, 1] = by_row_up
    key_in[rows, :STATE] = dot_left(d_scores, read, 0, 0)
    key_in[rows, STATE:] = dot_left(d_scores, write)


def finish(
    s,
    entry,
    values,
    keys,
    dts,
    sigs,
    params,
    g_b,
    y_in,
    d_in,
    key_in,
    row_sums,
    column_sums,
    mixed,
    d_val,
    d_key_high,
    d_key_low,
    d_raw_high,
    d_raw_low,
):
    channels = values.shape[1]
    heads = channels // HEAD
    rate, skip = params[1:2, :], params[2:3, :]
    spread = spread_matrix(channels)
    row_id, col_id = iota((ROWS, ROWS), 0), iota((ROWS, ROWS), 1)
    widen = lambda w: dot_left(w, spread)
    narrow = lambda w: dot_left(w, spread, 1, 1)
    skip_wide = widen(skip)
    rows = slice(s * ROWS, (s + 1) * ROWS)
    dt = dts[rows, :]
    log_decay, before, upto, total = decay_parts(dt, rate)
    x, g = values[rows, :].astype(F32), g_b.astype(F32)
    write, read = keys[rows, :STATE], keys[rows, STATE:]
    u_fwd, u_bwd = widen(jnp.exp(total - upto)), widen(jnp.exp(before))
    w_fwd, w_bwd = widen(jnp.exp(upto)), widen(jnp.exp(total - before))
    dt_wide = widen(dt)
    h_in, m_in, k_in, l_in = entry[0, s], entry[1, s], entry[2, s], entry[3, s]
    y_fwd = w_fwd * dot_right(read, h_in, 1, 1)
    y_bwd = w_bwd * dot_right(read, k_in, 1, 1)
    x_l = u_fwd * dot_right(write, l_in, 1, 1)
    x_m = u_bwd * dot_right(write, m_in, 1, 1)
    d_read = dot_both(w_fwd * g, h_in) + dot_both(w_bwd * g, k_in)
    d_write = dot_both(u_fwd * dt_wide * x, l_in) + dot_both(u_bwd * dt_wide * x, m_in)
    r_fwd, r_bwd = narrow(g * y_fwd), narrow(g * y_bwd)
    q_fwd, q_bwd = narrow(x * x_l), narrow(x * x_m)
    both = dot_right(spread, l_in * h_in + m_in * k_in)
    both = dot(jnp.ones((8, STATE), F32), both, 1, 1, precision=HIGHEST)[0:1]
    out = y_in[rows, :] + y_fwd + y_bwd + skip_wide * x
    mixed[...] = out.astype(BF16)
    d_val[rows, :] = (d_in[rows, :] + dt_wide * (x_l + x_m) + skip_wide * g).astype(BF16)
    sums = column_sums[s]
    picked = lambda at: dot_left(sums, where01((row_id == col_id + at) & (col_id < heads), BF16), 0, 0)
    d_dt = picked(0) + q_fwd + q_bwd
    d_upto = row_sums[s, 0] - picked(heads) + r_fwd - dt * q_fwd
    d_before = picked(2 * heads) - row_sums[s, 1] - r_bwd + dt * q_bwd
    d_total = jnp.sum(r_bwd + dt * q_fwd, 0, keepdims=True) + jnp.exp(total) * both
    d_log = dot(where01(row_id <= col_id), d_upto, precision=HIGHEST)
    d_log = d_log + dot(where01(row_id < col_id), d_before, precision=HIGHEST) + d_total
    d_raw_high[rows, :], d_raw_low[rows, :] = split((d_dt - rate * d_log) * sigs[rows, :])
    d_key_high[rows, :STATE], d_key_low[rows, :STATE] = split(d_write + key_in[rows, :STATE])
    d_key_high[rows, STATE:], d_key_low[rows, STATE:] = split(d_read + key_in[rows, STATE:])


def main_kernel(
    layers,
    ranks,
    complement_hbm,
    hidden_hbm,
    step_hbm,
    select_hbm,
    inner_hbm,
    cot_hbm,
    ccot_hbm,
    params,
    mixed,
    cmixed,
    first,
    second,
    complement,
    source,
    send,
    values,
    keys,
    dts,
    sigs,
    cot,
    ccot,
    inner,
    select,
    step,
    step_wide,
    entry,
    y_in,
    d_in,
    key_in,
    row_sums,
    column_sums,
    d_val,
    d_key_high,
    d_key_low,
    d_raw_high,
    d_raw_low,
    rows_in,
    sums,
    layered,
    scanned,
    before,
    members,
    term,
    shares,
    sems,
    gather_out,
    gather_in,
    up_out,
    up_in,
    back_out,
    back_in,
    spread_out,
    spread_in,
    share_out,
    share_in,
):
    fetches = [
        pltpu.make_async_copy(here, there, sems.at[i])
        for i, (here, there) in enumerate(
            (
                (complement_hbm, complement),
                (hidden_hbm, source.at[:ROWS]),
                (step_hbm, step),
                (select_hbm, select),
                (inner_hbm, inner),
                (cot_hbm, cot),
                (ccot_hbm, ccot),
            )
        )
    ]
    for fetch in fetches:
        fetch.start()
    me, rank = lax.axis_index("seq"), lax.axis_index("chan")
    channels = values.shape[1]
    heads = channels // HEAD
    width = term.shape[3]
    layer, member = me // ROW, lax.rem(me, ROW)
    down = member // 2
    each = heads // layers
    side = lambda j: layer * ROW + lax.rem(member + j, ROW)
    over = lambda j: lax.rem(layer + j, layers) * ROW + member
    across = lambda j: lax.rem(rank + j, ranks)
    place = {"device_id_type": pl.DeviceIdType.MESH}
    barrier = pltpu.get_barrier_semaphore()
    for j in range(1, ROW):
        pl.semaphore_signal(barrier, inc=1, device_id={"seq": side(j)}, **place)
    for j in range(1, layers):
        pl.semaphore_signal(barrier, inc=1, device_id={"seq": over(j)}, **place)
    for j in range(1, ranks):
        pl.semaphore_signal(barrier, inc=1, device_id={"chan": across(j)}, **place)
    project(fetches[:5], source, complement, inner, select, step, step_wide, params, values, keys, dts, sigs)

    def copy(here, there, sent, got, device):
        return pltpu.make_async_remote_copy(
            src_ref=here, dst_ref=there, send_sem=sent, recv_sem=got, device_id=device, **place
        )

    def gather(half, j):
        peer = lax.rem(member + j, ROW)
        there = rows_in.at[member, half]
        return copy(send.at[peer, half], there, gather_out.at[half, j], gather_in.at[half, j], {"seq": side(j)})

    def up(half, j):
        peer = lax.rem(layer + j, layers)
        there = layered.at[half, layer]
        return copy(sums.at[half, peer], there, up_out.at[half, j], up_in.at[half, j], {"seq": over(j)})

    def give_back(half, j):
        peer = lax.rem(layer + j, layers)
        there = before.at[half, layer]
        return copy(scanned.at[half, peer], there, back_out.at[half, j], back_in.at[half, j], {"seq": over(j)})

    def spread(half, j):
        peer = lax.rem(member + j, ROW)
        there = entry.at[member, half]
        return copy(members.at[half, peer], there, spread_out.at[half, j], spread_in.at[half, j], {"seq": side(j)})

    def share(half, j):
        there = shares.at[half, rank]
        return copy(term.at[half, across(j)], there, share_out.at[half, j], share_in.at[half, j], {"chan": across(j)})

    order = (2, 1, 3)
    far = tuple(j for j in (1, 7, 2, 6, 3, 5, 4) if j < layers)
    for s, g in ((0, cot), (1, ccot)):
        fetches[5 + s].wait()
        chunk_states(s, values, keys, dts, params[1:2, :], g[...], send)
        if s == 0:
            pl.semaphore_wait(barrier, ROW + layers + ranks - 3)
        for j in order:
            gather(s, j).start()
    rows_in[member] = send[member]
    column_sums[...] = jnp.zeros_like(column_sums)
    for s, g in ((0, cot), (1, ccot)):
        within_chunk(s, values, keys, dts, params[1:2, :], g[...], y_in, d_in, key_in, row_sums, column_sums)
    zero = jnp.zeros((HEAD // 8, 8, STATE), F32)

    def part(source, h, half):
        return rows_in[source, half, pl.ds(pl.multiple_of(h * HEAD, 8), HEAD), :].reshape(HEAD // 8, 8, STATE)

    def decay(source, h, half):
        return rows_in[source, half, pl.ds(pl.multiple_of(channels + 8 * h, 8), 8), :]

    def turned(lap, count):
        return lap + down * (count - 1 - 2 * lap)

    for half in range(2):
        for j in order:
            gather(half, j).wait_recv()

        def total(h, carry):
            state = zero
            through = jnp.ones((8, STATE), F32)
            for m in range(ROW):
                source = turned(m, ROW)
                slower = decay(source, h, half)
                state = state * slower[None] + part(source, h, half)
                through = through * slower
            sums[half, h // each, h % each, :HEAD, :] = state.reshape(HEAD, STATE)
            sums[half, h // each, h % each, HEAD:, :] = through
            return carry

        lax.fori_loop(0, heads, total, 0)
        for j in far:
            up(half, j).start()
        layered[half, layer] = sums[half, layer]
        for j in far:
            up(half, j).wait_recv()
        for e in range(each):

            def scan(lap, state):
                at = turned(lap, layers)
                scanned[half, at, e] = state.reshape(HEAD, STATE)
                slower = layered[half, at, e, HEAD:, :]
                return state * slower[None] + layered[half, at, e, :HEAD, :].reshape(HEAD // 8, 8, STATE)

            lax.fori_loop(0, layers, scan, zero)
        for j in far:
            give_back(half, j).start()
        before[half, layer] = scanned[half, layer]
        for j in far:
            give_back(half, j).wait_recv()

        def unfold(h, carry):
            state = before[half, h // each, h % each].reshape(HEAD // 8, 8, STATE)
            for m in range(ROW):
                target = turned(m, ROW)
                members[half, target, pl.ds(pl.multiple_of(h * HEAD, 8), HEAD), :] = state.reshape(HEAD, STATE)
                if m < ROW - 1:
                    state = state * decay(target, h, half)[None] + part(target, h, half)
            return carry

        lax.fori_loop(0, heads, unfold, 0)
        for j in order:
            spread(half, j).start()
        entry[member, half] = members[half, member]

    def chunk(half, block):
        rows = slice(half * ROWS, (half + 1) * ROWS)
        cols = pl.ds(pl.multiple_of(block * width, width), width)
        value = dot(d_val[rows, :], inner[cols, :], 1, 1)
        picked = select[cols, :]
        value = value + (dot(d_key_high[rows, :], picked, 1, 1) + dot(d_key_low[rows, :], picked, 1, 1))
        steps = step_wide[:, cols]
        return value + (dot(d_raw_high[rows, :], steps) + dot(d_raw_low[rows, :], steps))

    for s, g, out in ((0, cot, mixed), (1, ccot, cmixed)):
        for j in order:
            spread(s, j).wait_recv()
        finish(
            s,
            entry,
            values,
            keys,
            dts,
            sigs,
            params,
            g[...],
            y_in,
            d_in,
            key_in,
            row_sums,
            column_sums,
            out,
            d_val,
            d_key_high,
            d_key_low,
            d_raw_high,
            d_raw_low,
        )
        for j in range(1, ranks + 1):
            peer = across(j)
            term[s, peer] = chunk(s, ranks - 1 - peer if s else peer)
            if j < ranks:
                share(s, j).start()
    anti = anti_identity()
    for s in range(2):
        result = term[s, rank]
        for j in range(1, ranks):
            share(s, j).wait_recv()
            result = result + shares[s, across(ranks - j)]
        result = result.astype(BF16)
        if s == 0:
            first[...] = result
        else:
            blocks = width // FLIP
            for b in range(blocks):
                block = result[:, (blocks - 1 - b) * FLIP : (blocks - b) * FLIP]
                second[:, b * FLIP : (b + 1) * FLIP] = dot(block, anti).astype(BF16)
    for half in range(2):
        for j in order:
            gather(half, j).wait_send()
            spread(half, j).wait_send()
        for j in far:
            up(half, j).wait_send()
            give_back(half, j).wait_send()
        for j in range(1, ranks):
            share(half, j).wait_send()


def call(kernel, outs, args, scratch=(), far=0, **params):
    whole = pl.BlockSpec(memory_space=pltpu.VMEM)
    return pl.pallas_call(
        kernel,
        out_shape=[jax.ShapeDtypeStruct(shape, dtype) for shape, dtype in outs],
        in_specs=[pl.BlockSpec(memory_space=pltpu.HBM)] * far + [whole] * (len(args) - far),
        out_specs=[whole] * len(outs),
        scratch_shapes=list(scratch),
        compiler_params=pltpu.CompilerParams(vmem_limit_bytes=48 << 20, **params),
    )(*[pltpu.with_memory_space_constraint(a, pltpu.HBM) for a in args[:far]], *args[far:])


def local(hidden, complement, inner, select, step, bias, rate, skip, cot, ccot):
    shards, ranks = lax.axis_size("seq"), lax.axis_size("chan")
    heads = bias.shape[0]
    depth = hidden.shape[1]
    channels = heads * HEAD
    params = jnp.pad(jnp.stack([bias, rate, skip]), ((0, 5), (0, LANES - heads)))
    step = step.T
    layers = shards // ROW
    each = heads // layers
    width = depth // ranks
    dma = lambda *count: pltpu.SemaphoreType.DMA(count)
    wide = lambda *shape: pltpu.VMEM(shape, F32)
    narrow = lambda *shape: pltpu.VMEM(shape, BF16)
    return call(
        functools.partial(main_kernel, layers, ranks),
        [((ROWS, channels), BF16)] * 2 + [((ROWS, width), BF16)] * 2,
        (complement, hidden, step, select, inner, cot, ccot, params),
        [
            narrow(ROWS, depth),
            narrow(2 * ROWS, depth),
            wide(ROW, 2, channels + 8 * heads, STATE),
            narrow(2 * ROWS, channels),
            narrow(2 * ROWS, 2 * STATE),
            wide(2 * ROWS, LANES),
            wide(2 * ROWS, LANES),
            narrow(*cot.shape),
            narrow(*ccot.shape),
            narrow(*inner.shape),
            narrow(*select.shape),
            narrow(*step.shape),
            narrow(LANES, depth),
            wide(ROW, 2, channels, STATE),
            wide(2 * ROWS, channels),
            wide(2 * ROWS, channels),
            wide(2 * ROWS, 2 * STATE),
            wide(2, 2, ROWS, LANES),
            wide(2, ROWS, LANES),
            narrow(2 * ROWS, channels),
            narrow(2 * ROWS, 2 * STATE),
            narrow(2 * ROWS, 2 * STATE),
            narrow(2 * ROWS, LANES),
            narrow(2 * ROWS, LANES),
            wide(ROW, 2, channels + 8 * heads, STATE),
            wide(2, layers, each, HEAD + 8, STATE),
            wide(2, layers, each, HEAD + 8, STATE),
            wide(2, layers, each, HEAD, STATE),
            wide(2, layers, each, HEAD, STATE),
            wide(2, ROW, channels, STATE),
            wide(2, ranks, ROWS, width),
            wide(2, ranks, ROWS, width),
            dma(7),
            dma(2, ROW),
            dma(2, ROW),
            dma(2, layers),
            dma(2, layers),
            dma(2, layers),
            dma(2, layers),
            dma(2, ROW),
            dma(2, ROW),
            dma(2, ranks),
            dma(2, ranks),
        ],
        far=7,
        collective_id=1,
        has_side_effects=True,
    )


def solution(mesh):
    rows = P(("dp", "seq"), None)
    tiles = P(("dp", "seq"), "chan")
    in_specs = (rows, rows, P(None, "chan"), P(), P(None, "chan"), P("chan"), P("chan"), P("chan"), tiles, tiles)
    return jax.shard_map(
        local, mesh=mesh, in_specs=in_specs, out_specs=(tiles,) * 4, check_vma=False
    )
```
